128 devices in a mesh: gx: 16 (over x, y), gy: 8 (over z, core).
Axes of the slice: x: 4, y: 4, z: 4, core: 2. Of those that a mesh axis runs over, the one named last changes fastest.
Arguments:
- fields: float32 [4, 4, 640, 20480], P(None, None, 'gy', 'gx'), may hold values from -6 to 6
- owner: int32 [8192, 1], P(('gx', 'gy')), may hold values from 0 to 127; in each aligned block of 64 rows (0 to 63, 64 to 127, ...) at most 2 rows name the same one
Outputs:
- received: float32 [32768, 640], P(('gx', 'gy'))
The draws below stay inside these ranges and needn't reach their ends.
Inputs may be any that keep to these rules, and one draw needn't show every extreme that they name: Among the blocks of one device, no owner is named more than 2 times, a bound that some block reaches.
All inputs are finite; a program needn't handle non-finite values.
Results may differ from the reference program's by a relative error of at most 0.0001.
Values sent between devices are 32-bit elements; how exact they have to be, the bound alone decides.
A program may use at most 256 MiB of HBM per device.

```python
import math
import jax
import jax.numpy as jnp
import numpy as np
from jax import lax

LEV = 4
BLK = 4
NX = 20480
NY = 640
NBX = 32
NBY = 2
NB_DEV = 64
NBLOCKS = 8192
PAIRCAP = 2
PAY = 640
SLOTS = 32768
N_GX = 16
N_GY = 8
DEVICES = 128


def steps_of(key, shape, pieces, least, largest):
    loudness, own = 1.0, jax.random.fold_in(key, 6)
    for dim, shards_of in pieces:
        heights = jnp.exp(jax.random.uniform(jax.random.fold_in(own, dim), (shards_of,), jnp.float32, least / len(pieces), largest / len(pieces)))
        loudness = loudness * jnp.repeat(heights, shape[dim] // shards_of).reshape([-1 if axis == dim else 1 for axis in range(len(shape))])
    return loudness


def deal_out(key, own, number, rows, count, top, limit, skew):
    sequence = jax.random.permutation(key, count)
    heavy_load, ordinary = load_shares(count, rows * top, limit, skew, True), load_shares(count, rows * top, limit, skew, False)
    places = jnp.arange(count)

    def named(lengths, turn):
        used = int((lengths > 0).sum())
        fixed = max(1, used // 4)
        moved = fixed + (places - fixed + turn * (used - fixed)) % max(1, count - fixed)
        return jnp.zeros((count,), jnp.int32).at[sequence[jnp.where(places < fixed, places, moved)]].set(jnp.asarray(lengths, jnp.int32))

    lengths = jnp.where(number % 4 == 0, named(heavy_load, number // 4), named(ordinary, number - number // 4 - 1))
    mixed = jax.random.permutation(jax.random.fold_in(own, 3), count)
    source_of, sink = mixed[0:count // 2 * 2:2], mixed[1:count // 2 * 2:2]
    room = jnp.minimum(lengths[source_of] - 1, limit - lengths[sink]) // 2
    room = jnp.where((source_of == sequence[0]) | (sink == sequence[0]) | (lengths[sink] == 0), 0, jnp.maximum(room, 0))
    moved = jax.random.randint(jax.random.fold_in(own, 4), (count // 2,), 0, 1 << 20) % (room + 1)
    lengths = lengths.at[source_of].add(-moved).at[sink].add(moved)
    items = jnp.searchsorted(jnp.cumsum(lengths), jnp.arange(rows * top), side="right").astype(jnp.int32)
    table = items.reshape(top, rows).T
    table = table[jax.random.permutation(jax.random.fold_in(own, 1), rows)]
    turn = jax.random.randint(jax.random.fold_in(own, 2), (rows, 1), 0, top)
    return jnp.take_along_axis(table, (jnp.arange(top)[None, :] + turn) % top, axis=1)


def load_shares(amount, total, reach, slope, full):
    portions = [(1 << 20) // math.isqrt(standing ** slope) + 1 for standing in range(1, amount + 1)]
    largest = reach if full else min(reach, max(-(-total // amount), total * portions[0] // sum(portions)))
    least = 1 if total - largest >= amount - 1 else 0
    holding, spare = [largest] + [least] * (amount - 1), total - largest - least * (amount - 1)
    while spare > 0:
        candidates = [i for i in range(1, amount) if holding[i] < largest] or [i for i in range(1, amount) if holding[i] < reach]
        pool, budget = sum([portions[i] for i in candidates]), spare
        for i in candidates:
            extra = min(reach - holding[i], max(1, budget * portions[i] // pool), spare)
            holding[i] = holding[i] + extra
            spare = spare - extra
    return np.array(holding)


def centred(rng, dims, deviation, most, pieces=(), held_as=jnp.bfloat16):
    factor_of = steps_of(rng, dims, pieces, -0.22, 0.18) if pieces else 1.0
    entries = jax.random.normal(rng, dims, jnp.float32) * deviation * factor_of
    return jnp.minimum(jnp.maximum(entries, -most), most).astype(held_as)


def setup_inputs(seed: int = 0) -> dict:
    arg_keys = jax.random.split(jax.random.key(seed), 3)
    fields = centred(arg_keys[0], (4, LEV, NY, NX), 1.0, 6.0, ((2, 8), (3, 16)), jnp.float32)
    owner_keys = jax.random.split(jax.random.fold_in(arg_keys[1], 1), NBLOCKS // NB_DEV)
    owner_turns = jax.random.permutation(jax.random.fold_in(arg_keys[1], 3), NBLOCKS // NB_DEV)
    owner = jax.vmap(lambda own, number: deal_out(jax.random.fold_in(arg_keys[1], 2), own, number, NB_DEV, DEVICES, 1, PAIRCAP, 2))(owner_keys, owner_turns).reshape((NBLOCKS, 1))
    return {"fields": fields, "owner": owner}


SIGMA_CELLS = 2.8867513
PRODUCT_PAIRS = ((0, 0), (0, 1), (0, 2), (0, 3), (1, 1), (1, 2), (1, 3), (2, 2), (2, 3), (3, 3))


def gauss_taps():
    spread = jnp.arange(21, dtype=jnp.float32) - 10.0
    values = jnp.exp(-spread * spread / (2.0 * SIGMA_CELLS * SIGMA_CELLS))
    return values / jnp.sum(values)


def filter_last(field, weights):
    length = field.shape[-1]
    coarse_len = length // 10
    padded = jnp.concatenate([field[..., length - 5:], field, field[..., :15]], axis=-1)
    groups = padded.reshape(field.shape[:-1] + (coarse_len + 2, 10))
    lead_part = jnp.sum(groups[..., :coarse_len, :] * weights[:10], axis=-1)
    next_part = jnp.sum(groups[..., 1:coarse_len + 1, :] * weights[10:20], axis=-1)
    tail_part = groups[..., 2:coarse_len + 2, 0] * weights[20]
    return lead_part + next_part + tail_part


def filter_plane(field, weights):
    along_east = filter_last(field, weights)
    return jnp.swapaxes(filter_last(jnp.swapaxes(along_east, -1, -2), weights), -1, -2)


def reference(fields, owner):
    weights = gauss_taps()

    def one_level(level_index):
        level_field = lax.dynamic_index_in_dim(fields, level_index, 1, keepdims=False)
        components = [level_field[c] for c in range(4)]
        coarse_means = [filter_plane(c, weights) for c in components]
        pair_terms = []
        for first_idx, second_idx in PRODUCT_PAIRS:
            product = filter_plane(components[first_idx] * components[second_idx], weights)
            pair_terms.append(product - coarse_means[first_idx] * coarse_means[second_idx])
        return jnp.stack(pair_terms)

    stresses = lax.map(one_level, jnp.arange(LEV, dtype=jnp.int32))
    stresses = jnp.moveaxis(stresses, 0, 1)
    blocks = stresses.reshape(10, LEV, N_GY, NBY, BLK, N_GX, NBX, BLK)
    blocks = jnp.transpose(blocks, (5, 2, 3, 6, 0, 1, 4, 7)).reshape(NBLOCKS, PAY)
    destination = owner[:, 0].reshape(DEVICES, NB_DEV)
    onehot = (destination[:, :, None] == jnp.arange(DEVICES, dtype=jnp.int32)[None, None, :]).astype(jnp.int32)
    before = jnp.cumsum(onehot, axis=1) - onehot
    place_rank = jnp.sum(before * onehot, axis=2)
    source = jnp.arange(DEVICES, dtype=jnp.int32)[:, None]
    target = destination * (DEVICES * PAIRCAP) + source * PAIRCAP + place_rank
    received = jnp.zeros((SLOTS, PAY), jnp.float32).at[target.reshape(-1)].set(blocks)
    return received
```

```python
import functools

import jax
import jax.numpy as jnp
import numpy as np
from jax import lax
from jax.experimental import pallas as pl
from jax.experimental.pallas import tpu as pltpu
from jax.sharding import PartitionSpec as P

MESH = pl.DeviceIdType.MESH
BLK = 4
LEV = 4
RATIO = 10
TAPS = 21
SIGMA_CELLS = 2.8867513
PAIRS = ((0, 0), (0, 1), (0, 2), (0, 3), (1, 1), (1, 2), (1, 3), (2, 2), (2, 3), (3, 3))
NF = 4 + len(PAIRS)
FL = NF * LEV
MAIN = FL * 8
SIDE = 64
ROWS = MAIN + 2 * SIDE
KC = 256
ORDER = (0, 3, 1, 2)
LANE_LAST = 63


def gauss_taps():
    spread = np.arange(TAPS, dtype=np.float32) - np.float32(10.0)
    values = np.exp(-spread * spread / np.float32(2.0 * SIGMA_CELLS * SIGMA_CELLS)).astype(np.float32)
    return (values / values.sum(dtype=np.float32)).astype(np.float32)


def east_matrix(length, taps):
    coarse = length // RATIO
    w = np.zeros((length, 256), np.float32)
    cols = [(128, coarse), (128 + LANE_LAST, -1)]
    for lane in range(128):
        cols.append((lane, 4 * (lane % 32) + ORDER[lane // 32]))
    for lane, j in cols:
        for t in range(TAPS):
            x = RATIO * j - 5 + t
            if 0 <= x < length:
                w[x, lane] = taps[t]
    return w


def block_matrix():
    m = np.zeros((256, 256), np.float32)
    for grp in range(4):
        for kl in range(8):
            for i in range(8):
                by, r = divmod(i, 4)
                m[grp * 64 + kl * 8 + i, by * 128 + kl * 16 + r * 4 + ORDER[grp]] = 1.0
    return m


def split3(x):
    hi = x.astype(jnp.bfloat16)
    rest = x - hi.astype(jnp.float32)
    mid = rest.astype(jnp.bfloat16)
    lo = (rest - mid.astype(jnp.float32)).astype(jnp.bfloat16)
    return hi, mid, lo


def iota(shape, dim):
    return lax.broadcasted_iota(jnp.int32, shape, dim)


def north_parts(v, g):
    q5, q0 = g[5] * v[0], g[0] * v[5]
    a = q5 + g[10] * v[5] + g[9] * (v[4] + v[6]) + g[8] * (v[3] + v[7]) + g[7] * (v[2] + v[8]) + g[6] * (v[1] + v[9])
    b = q0 + g[1] * v[6] + g[2] * v[7] + g[3] * v[8] + g[4] * v[9]
    c = q5 + q0 + g[4] * v[1] + g[3] * v[2] + g[2] * v[3] + g[1] * v[4]
    return a, b, c


def north_chunk(f_ref, kc, x_ref, g):
    row = iota((8, 128), 0)
    for lev in range(LEV):
        for lt in range(KC // 128):
            lanes = slice(lt * 128, lt * 128 + 128)
            x = [[f_ref[kc * (KC // 128) + lt, a, lev, pl.ds(o, 8, stride=RATIO), :] for o in range(RATIO)] for a in range(4)]
            for f in range(NF):
                if f < 4:
                    v = x[f]
                else:
                    p, q = PAIRS[f - 4]
                    v = [x[p][o] * x[q][o] for o in range(RATIO)]
                a, b, c = north_parts(v, g)
                b = pltpu.roll(b, 1, 0)
                c = pltpu.roll(c, 7, 0)
                fl = f * LEV + lev
                x_ref[fl * 8 : fl * 8 + 8, lanes] = a + jnp.where(row == 0, 0.0, b) + jnp.where(row == 7, 0.0, c)
                x_ref[MAIN + fl : MAIN + fl + 1, lanes] = b[0:1]
                x_ref[MAIN + SIDE + fl : MAIN + SIDE + fl + 1, lanes] = c[7:8]


def selector(owner_ref):
    own = owner_ref[...].astype(jnp.float32)
    row = jnp.broadcast_to(jnp.concatenate([own, own], axis=1), (128, 128))
    col = row.T[:64]
    before = (col == row[:64]) & (iota((64, 128), 0) < (iota((64, 128), 1) & 63))
    rank = jnp.sum(before.astype(jnp.float32), axis=0, keepdims=True)
    slot = row[0:1] * 2.0 + rank
    where = iota((256, 128), 0).astype(jnp.float32)
    return (where == slot).astype(jnp.bfloat16)


def kernel(n_gx, n_gy, g, f_hbm, w_hbm, m_hbm, o_hbm, dst, f_ref, w_ref, m_ref, owner_ref, x_ref, t_ref, s_ref, src,
           edge, corner, r_next, r_prev, r_side, r_corner, fsem, wsem, msem, osem, ssem, rsem, hsend, hrecv, lsem):
    n = n_gx * n_gy
    gx, gy = lax.axis_index("gx"), lax.axis_index("gy")
    me = gx * n_gy + gy
    steps = w_ref.shape[0]
    per = KC // 128

    def f_copy(lt):
        return pltpu.make_async_copy(f_hbm.at[:, :, :, pl.ds(pl.multiple_of(lt * 128, 128), 128)], f_ref.at[lt], fsem.at[lt])

    def w_copy(kc):
        return pltpu.make_async_copy(w_hbm.at[pl.ds(pl.multiple_of(kc * KC, KC), KC)], w_ref.at[kc], wsem.at[kc])

    for kc in range(steps):
        for lt in range(per):
            f_copy(kc * per + lt).start()
        w_copy(kc).start()
    m_copy = pltpu.make_async_copy(m_hbm, m_ref, msem)
    m_copy.start()
    o_copy = pltpu.make_async_copy(o_hbm, owner_ref, osem)
    o_copy.start()

    barrier = pltpu.get_barrier_semaphore()

    def greet(k, carry):
        d = lax.rem(me + k, n)
        pl.semaphore_signal(barrier, inc=1, device_id=(d // n_gy, lax.rem(d, n_gy)), device_id_type=MESH)
        return carry

    lax.fori_loop(1, n, greet, 0)
    x_ref[MAIN:ROWS] = jnp.zeros((2 * SIDE, KC), jnp.float32)
    t_ref[...] = jnp.zeros_like(t_ref)

    def chunk(kc, carry):
        for lt in range(per):
            f_copy(kc * per + lt).wait()
        north_chunk(f_ref, kc, x_ref, g)
        w_copy(kc).wait()
        t_ref[...] += jnp.dot(
            x_ref[...], w_ref[kc], precision=lax.Precision.HIGHEST, preferred_element_type=jnp.float32)
        return carry

    lax.fori_loop(0, steps, chunk, 0)

    lane = iota((8, 128), 1)
    row = iota((8, 128), 0)
    keep = (lane == 0) | (lane == LANE_LAST)
    packed = jnp.zeros((8, 128), jnp.float32)
    for fl in range(FL):
        v = jnp.where(keep, t_ref[fl * 8 : fl * 8 + 8, 128:256], 0.0)
        packed = packed + (pltpu.roll(v, fl, 1) if fl else v)
    edge[...] = packed
    turned = t_ref[MAIN:ROWS, 128:256].T
    corner[...] = jnp.where(row == 0, turned[0:1], turned[LANE_LAST : LANE_LAST + 1])

    pl.semaphore_wait(barrier, n - 1)
    east, west = lax.rem(gx + 1, n_gx), lax.rem(gx + n_gx - 1, n_gx)
    up, down = lax.rem(gy + 1, n_gy), lax.rem(gy + n_gy - 1, n_gy)
    moves = (
        (t_ref.at[MAIN : MAIN + SIDE, 0:128], r_next, (gx, up)),
        (t_ref.at[MAIN + SIDE : ROWS, 0:128], r_prev, (gx, down)),
        (edge, r_side.at[0], (east, gy)),
        (edge, r_side.at[1], (west, gy)),
        (corner, r_corner.at[0], (east, up)),
        (corner, r_corner.at[1], (east, down)),
        (corner, r_corner.at[2], (west, up)),
        (corner, r_corner.at[3], (west, down)),
    )
    copies = [
        pltpu.make_async_remote_copy(s, d, hsend.at[i], hrecv.at[i], device_id=to, device_id_type=MESH)
        for i, (s, d, to) in enumerate(moves)
    ]
    for copy in copies:
        copy.start()
    o_copy.wait()
    sel = selector(owner_ref)
    for copy in copies:
        copy.wait()

    side = jnp.where(lane < 60, r_side[0], r_side[1])
    c0, c1, c2, c3 = r_corner[0], r_corner[1], r_corner[2], r_corner[3]
    first = (lane < FL)
    secnd = (lane >= LANE_LAST) & (lane < LANE_LAST + FL)
    side = side + jnp.where(first & (row == 0), c0, 0.0)
    side = side + jnp.where(first & (row == 7), pltpu.roll(jnp.broadcast_to(c1[0:1], (8, 128)), 64, 1), 0.0)
    side = side + jnp.where(secnd & (row == 0), pltpu.roll(jnp.broadcast_to(c2[1:2], (8, 128)), LANE_LAST, 1), 0.0)
    side = side + jnp.where(secnd & (row == 7), pltpu.roll(jnp.broadcast_to(c3[1:2], (8, 128)), 127, 1), 0.0)
    for lev in range(LEV):
        m = []
        for f in range(NF):
            fl = f * LEV + lev
            v = t_ref[fl * 8 : fl * 8 + 8, 0:128]
            v = v + jnp.where(row == 0, r_next[fl : fl + 1], 0.0) + jnp.where(row == 7, r_prev[fl : fl + 1], 0.0)
            m.append(v + jnp.where(keep, pltpu.roll(side, 128 - fl, 1) if fl else side, 0.0))
        for k, (p, q) in enumerate(PAIRS):
            at = (k * LEV + lev) * 8
            s_ref[at : at + 8] = m[4 + k] - m[p] * m[q]
    half = iota((32, 128), 1) < 64
    tiles = []
    for tt in range(3):
        st = s_ref[tt * 128 : tt * 128 + 128].T
        rt = pltpu.roll(st, 64, 1)
        left = [st[i * 32 : i * 32 + 32] for i in range(4)]
        right = [rt[i * 32 : i * 32 + 32] for i in range(4)]
        tiles.append((jnp.where(half, left[0], right[1]), jnp.where(half, left[2], right[3])))
        tiles.append((jnp.where(half, right[0], left[1]), jnp.where(half, right[2], left[3])))
    tiles = tiles[:5]
    lhs = jnp.concatenate([jnp.concatenate([a, b], axis=1) for a, b in tiles], axis=0)
    lhs = jnp.concatenate(split3(lhs), axis=0)
    m_copy.wait()
    o = jnp.dot(lhs, m_ref[...], preferred_element_type=jnp.float32).astype(jnp.bfloat16)
    pay = []
    for part in range(3):
        for by in range(2):
            at = part * 160
            pay.append(jnp.concatenate(
                [o[at + gg * 32 : at + gg * 32 + 32, by * 128 : by * 128 + 128] for gg in range(5)], axis=1))
    pair = jnp.concatenate(pay[0:4], axis=0)
    one = jnp.concatenate(pay[4:6], axis=0)
    out = jnp.dot(sel, pair, preferred_element_type=jnp.float32)
    out = out + jnp.dot(sel[:, :64], one, preferred_element_type=jnp.float32)
    src[...] = out.reshape(n, 2, 640)

    own = pltpu.make_async_copy(src.at[me], dst.at[me], lsem)
    own.start()

    def send(k, carry):
        d = lax.rem(me + k, n)
        pltpu.make_async_remote_copy(
            src.at[d], dst.at[me], ssem, rsem, device_id=(d // n_gy, lax.rem(d, n_gy)), device_id_type=MESH
        ).start()
        return carry

    lax.fori_loop(1, n, send, 0)
    own.wait()
    rest = pl.ds(0, n - 1)
    pltpu.make_async_copy(src.at[rest], dst.at[rest], ssem).wait()
    pltpu.make_async_copy(src.at[rest], dst.at[rest], rsem).wait()


def per_device(fields, owner):
    n_gx, n_gy = lax.axis_size("gx"), lax.axis_size("gy")
    n = n_gx * n_gy
    taps = gauss_taps()
    g = [float(x) for x in taps]
    length = fields.shape[-1]
    weights = jnp.asarray(east_matrix(length, taps))
    blocks = jnp.asarray(block_matrix(), jnp.bfloat16)
    f32 = jnp.float32
    out = pl.pallas_call(
        functools.partial(kernel, n_gx, n_gy, g),
        out_shape=jax.ShapeDtypeStruct((n, 2, 640), f32),
        in_specs=[
            pl.BlockSpec(memory_space=pltpu.HBM),
            pl.BlockSpec(memory_space=pltpu.HBM),
            pl.BlockSpec(memory_space=pltpu.HBM),
            pl.BlockSpec(memory_space=pltpu.HBM),
        ],
        out_specs=pl.BlockSpec(memory_space=pltpu.VMEM),
        scratch_shapes=[
            pltpu.VMEM((length // 128, 4, LEV, 80, 128), f32),
            pltpu.VMEM((length // KC, KC, 256), f32),
            pltpu.VMEM((256, 256), jnp.bfloat16),
            pltpu.VMEM((1, 64), jnp.int32),
            pltpu.VMEM((ROWS, KC), f32),
            pltpu.VMEM((ROWS, 256), f32),
            pltpu.VMEM((384, 128), f32),
            pltpu.VMEM((n, 2, 640), f32),
            pltpu.VMEM((8, 128), f32),
            pltpu.VMEM((8, 128), f32),
            pltpu.VMEM((SIDE, 128), f32),
            pltpu.VMEM((SIDE, 128), f32),
            pltpu.VMEM((2, 8, 128), f32),
            pltpu.VMEM((4, 8, 128), f32),
            pltpu.SemaphoreType.DMA((length // 128,)),
            pltpu.SemaphoreType.DMA((length // KC,)),
            pltpu.SemaphoreType.DMA,
            pltpu.SemaphoreType.DMA,
            pltpu.SemaphoreType.DMA,
            pltpu.SemaphoreType.DMA,
            pltpu.SemaphoreType.DMA((8,)),
            pltpu.SemaphoreType.DMA((8,)),
            pltpu.SemaphoreType.DMA,
        ],
        compiler_params=pltpu.CompilerParams(
            collective_id=0, has_side_effects=True, vmem_limit_bytes=24 << 20
        ),
    )(*(pltpu.with_memory_space_constraint(x, pltpu.HBM) for x in (fields, weights, blocks, owner.reshape(1, 64))))
    return out.reshape(n * 2, 640)


def solution(mesh):
    placed = (P(None, None, "gy", "gx"), P(("gx", "gy"), None))
    return jax.shard_map(
        per_device, mesh=mesh, in_specs=placed, out_specs=P(("gx", "gy"), None), check_vma=False
    )
```

```python
import functools

import jax
import jax.numpy as jnp
import numpy as np
from jax import lax
from jax.experimental import pallas as pl
from jax.experimental.pallas import tpu as pltpu
from jax.sharding import PartitionSpec as P

MESH = pl.DeviceIdType.MESH
BLK = 4
LEV = 4
RATIO = 10
TAPS = 21
SIGMA_CELLS = 2.8867513
PAIRS = ((0, 0), (0, 1), (0, 2), (0, 3), (1, 1), (1, 2), (1, 3), (2, 2), (2, 3), (3, 3))
ROUND_A = tuple((a, None) for a in range(4)) + PAIRS[:4]
ROUND_B = PAIRS[4:]
SIDE = 32
KC = 256
ORDER = (0, 3, 1, 2)
LANE_LAST = 63


def gauss_taps():
    spread = np.arange(TAPS, dtype=np.float32) - np.float32(10.0)
    values = np.exp(-spread * spread / np.float32(2.0 * SIGMA_CELLS * SIGMA_CELLS)).astype(np.float32)
    return (values / values.sum(dtype=np.float32)).astype(np.float32)


def east_matrix(length, taps):
    coarse = length // RATIO
    w = np.zeros((length, 256), np.float32)
    cols = [(128, coarse), (128 + LANE_LAST, -1)]
    for lane in range(128):
        cols.append((lane, 4 * (lane % 32) + ORDER[lane // 32]))
    for lane, j in cols:
        for t in range(TAPS):
            x = RATIO * j - 5 + t
            if 0 <= x < length:
                w[x, lane] = taps[t]
    return w


def block_matrix():
    m = np.zeros((256, 256), np.float32)
    for grp in range(4):
        for kl in range(8):
            for i in range(8):
                by, r = divmod(i, 4)
                m[grp * 64 + kl * 8 + i, by * 128 + kl * 16 + r * 4 + ORDER[grp]] = 1.0
    return m


def split3(x):
    hi = x.astype(jnp.bfloat16)
    rest = x - hi.astype(jnp.float32)
    mid = rest.astype(jnp.bfloat16)
    lo = (rest - mid.astype(jnp.float32)).astype(jnp.bfloat16)
    return hi, mid, lo


def iota(shape, dim):
    return lax.broadcasted_iota(jnp.int32, shape, dim)


def north_parts(v, g):
    q5, q0 = g[5] * v[0], g[0] * v[5]
    a = q5 + g[10] * v[5] + g[9] * (v[4] + v[6]) + g[8] * (v[3] + v[7]) + g[7] * (v[2] + v[8]) + g[6] * (v[1] + v[9])
    b = q0 + g[1] * v[6] + g[2] * v[7] + g[3] * v[8] + g[4] * v[9]
    c = q5 + q0 + g[4] * v[1] + g[3] * v[2] + g[2] * v[3] + g[1] * v[4]
    return a, b, c


def north_chunk(fields, f_ref, kc, x_ref, g):
    row = iota((8, 128), 0)
    main = len(fields) * LEV * 8
    used = sorted({a for pair in fields for a in pair if a is not None})
    for lev in range(LEV):
        for lt in range(KC // 128):
            lanes = slice(lt * 128, lt * 128 + 128)
            x = {a: [f_ref[kc * (KC // 128) + lt, a, lev, pl.ds(o, 8, stride=RATIO), :] for o in range(RATIO)] for a in used}
            for f, (p, q) in enumerate(fields):
                v = x[p] if q is None else [x[p][o] * x[q][o] for o in range(RATIO)]
                a, b, c = north_parts(v, g)
                b = pltpu.roll(b, 1, 0)
                c = pltpu.roll(c, 7, 0)
                fl = f * LEV + lev
                x_ref[fl * 8 : fl * 8 + 8, lanes] = a + jnp.where(row == 0, 0.0, b) + jnp.where(row == 7, 0.0, c)
                x_ref[main + fl : main + fl + 1, lanes] = b[0:1]
                x_ref[main + SIDE + fl : main + SIDE + fl + 1, lanes] = c[7:8]


def selector(owner_ref):
    own = owner_ref[...].astype(jnp.float32)
    row = jnp.broadcast_to(jnp.concatenate([own, own], axis=1), (128, 128))
    col = row.T[:64]
    before = (col == row[:64]) & (iota((64, 128), 0) < (iota((64, 128), 1) & 63))
    rank = jnp.sum(before.astype(jnp.float32), axis=0, keepdims=True)
    slot = row[0:1] * 2.0 + rank
    where = iota((256, 128), 0).astype(jnp.float32)
    return (where == slot).astype(jnp.bfloat16)


def pack_rim(count, t_ref, edge, corner):
    lane = iota((8, 128), 1)
    row = iota((8, 128), 0)
    keep = (lane == 0) | (lane == LANE_LAST)
    packed = jnp.zeros((8, 128), jnp.float32)
    for fl in range(count):
        v = jnp.where(keep, t_ref[fl * 8 : fl * 8 + 8, 128:256], 0.0)
        packed = packed + (pltpu.roll(v, fl, 1) if fl else v)
    edge[...] = packed
    rows = count * 8 + 2 * SIDE
    turned = t_ref[rows - 128 : rows, 128:256].T
    corner[...] = jnp.where(row == 0, turned[0:1], turned[LANE_LAST : LANE_LAST + 1])


def rim_copies(n_gx, n_gy, gx, gy, count, t_ref, edge, corner, r_next, r_prev, r_side, r_corner, hsend, hrecv):
    east, west = lax.rem(gx + 1, n_gx), lax.rem(gx + n_gx - 1, n_gx)
    up, down = lax.rem(gy + 1, n_gy), lax.rem(gy + n_gy - 1, n_gy)
    main = count * 8
    moves = (
        (t_ref.at[main : main + SIDE, 0:128], r_next, (gx, up)),
        (t_ref.at[main + SIDE : main + 2 * SIDE, 0:128], r_prev, (gx, down)),
        (edge, r_side.at[0], (east, gy)),
        (edge, r_side.at[1], (west, gy)),
        (corner, r_corner.at[0], (east, up)),
        (corner, r_corner.at[1], (east, down)),
        (corner, r_corner.at[2], (west, up)),
        (corner, r_corner.at[3], (west, down)),
    )
    return [
        pltpu.make_async_remote_copy(s, d, hsend.at[i], hrecv.at[i], device_id=to, device_id_type=MESH)
        for i, (s, d, to) in enumerate(moves)
    ]


def rim_added(count, t_ref, r_next, r_prev, r_side, r_corner):
    lane = iota((8, 128), 1)
    row = iota((8, 128), 0)
    keep = (lane == 0) | (lane == LANE_LAST)
    side = jnp.where(lane < 60, r_side[0], r_side[1])
    first = lane < count
    secnd = (lane >= LANE_LAST) & (lane < LANE_LAST + count)
    corners = ((first, 0, 0, 64), (first, 7, 0, 32), (secnd, 0, 1, 127), (secnd, 7, 1, 95))
    for i, (lanes, at, got, turn) in enumerate(corners):
        v = jnp.broadcast_to(r_corner[i, got : got + 1], (8, 128))
        side = side + jnp.where(lanes & (row == at), pltpu.roll(v, turn, 1), 0.0)
    out = []
    for fl in range(count):
        v = t_ref[fl * 8 : fl * 8 + 8, 0:128]
        v = v + jnp.where(row == 0, r_next[fl : fl + 1], 0.0) + jnp.where(row == 7, r_prev[fl : fl + 1], 0.0)
        out.append(v + jnp.where(keep, pltpu.roll(side, 128 - fl, 1) if fl else side, 0.0))
    return out


def slots(groups, sel, s_ref, m_ref):
    half = iota((32, 128), 1) < 64
    tiles = []
    for tt in range((groups + 1) // 2):
        st = s_ref[tt * 128 : tt * 128 + 128].T
        rt = pltpu.roll(st, 64, 1)
        left = [st[i * 32 : i * 32 + 32] for i in range(4)]
        right = [rt[i * 32 : i * 32 + 32] for i in range(4)]
        tiles.append((jnp.where(half, left[0], right[1]), jnp.where(half, left[2], right[3])))
        tiles.append((jnp.where(half, right[0], left[1]), jnp.where(half, right[2], left[3])))
    tiles = tiles[:groups]
    lhs = jnp.concatenate([jnp.concatenate([a, b], axis=1) for a, b in tiles], axis=0)
    lhs = jnp.concatenate(split3(lhs), axis=0)
    o = jnp.dot(lhs, m_ref[...], preferred_element_type=jnp.float32).astype(jnp.bfloat16)
    pay = []
    for part in range(3):
        for by in range(2):
            at = part * groups * 32
            pay.append(jnp.concatenate(
                [o[at + gg * 32 : at + gg * 32 + 32, by * 128 : by * 128 + 128] for gg in range(groups)], axis=1))
    out = jnp.dot(sel, jnp.concatenate(pay[0:4], axis=0), preferred_element_type=jnp.float32)
    return out + jnp.dot(sel[:, :64], jnp.concatenate(pay[4:6], axis=0), preferred_element_type=jnp.float32)


def kernel(n_gx, n_gy, g, f_hbm, w_hbm, m_hbm, o_hbm, out_ref, f_ref, w_ref, m_ref, owner_ref, x_a, x_b, t_a, t_b,
           mean_ref, s_a, s_b, src_a, src_b, dst_a, dst_b, edge, corner, r_next, r_prev, r_side, r_corner,
           fsem, wsem, msem, osem, ssem, rsem, hsend, hrecv, lsem):
    n = n_gx * n_gy
    gx, gy = lax.axis_index("gx"), lax.axis_index("gy")
    me = gx * n_gy + gy
    steps = w_ref.shape[0]
    per = KC // 128
    count_a, count_b = len(ROUND_A) * LEV, len(ROUND_B) * LEV

    def f_copy(lt):
        return pltpu.make_async_copy(f_hbm.at[:, :, :, pl.ds(pl.multiple_of(lt * 128, 128), 128)], f_ref.at[lt], fsem.at[lt])

    def w_copy(kc):
        return pltpu.make_async_copy(w_hbm.at[pl.ds(pl.multiple_of(kc * KC, KC), KC)], w_ref.at[kc], wsem.at[kc])

    for kc in range(steps):
        for lt in range(per):
            f_copy(kc * per + lt).start()
        w_copy(kc).start()
    m_copy = pltpu.make_async_copy(m_hbm, m_ref, msem)
    m_copy.start()
    o_copy = pltpu.make_async_copy(o_hbm, owner_ref, osem)
    o_copy.start()

    barrier = pltpu.get_barrier_semaphore()

    def greet(k, carry):
        d = lax.rem(me + k, n)
        pl.semaphore_signal(barrier, inc=1, device_id=(d // n_gy, lax.rem(d, n_gy)), device_id_type=MESH)
        return carry

    lax.fori_loop(1, n, greet, 0)

    def local(fields, x_ref, t_ref, fresh):
        main = len(fields) * LEV * 8
        x_ref[main : main + 2 * SIDE] = jnp.zeros((2 * SIDE, KC), jnp.float32)
        t_ref[...] = jnp.zeros_like(t_ref)

        def chunk(kc, carry):
            if fresh:
                for lt in range(per):
                    f_copy(kc * per + lt).wait()
            north_chunk(fields, f_ref, kc, x_ref, g)
            if fresh:
                w_copy(kc).wait()
            t_ref[...] += jnp.dot(
                x_ref[...], w_ref[kc], precision=lax.Precision.HIGHEST, preferred_element_type=jnp.float32)
            return carry

        lax.fori_loop(0, steps, chunk, 0)

    def rims(i, count, t_ref):
        bufs = (edge, corner, r_next, r_prev, r_side, r_corner, hsend, hrecv)
        return rim_copies(n_gx, n_gy, gx, gy, count, t_ref, *(b.at[i] for b in bufs))

    def hand_over(i, src, dst):
        own = pltpu.make_async_copy(src.at[me], dst.at[me], lsem.at[i])
        own.start()

        def send(k, carry):
            d = lax.rem(me + k, n)
            pltpu.make_async_remote_copy(
                src.at[d], dst.at[me], ssem.at[i], rsem.at[i],
                device_id=(d // n_gy, lax.rem(d, n_gy)), device_id_type=MESH,
            ).start()
            return carry

        lax.fori_loop(1, n, send, 0)
        return own

    local(ROUND_A, x_a, t_a, True)
    pack_rim(count_a, t_a, edge.at[0], corner.at[0])
    pl.semaphore_wait(barrier, n - 1)
    copies_a = rims(0, count_a, t_a)
    for copy in copies_a:
        copy.start()
    local(ROUND_B, x_b, t_b, False)
    pack_rim(count_b, t_b, edge.at[1], corner.at[1])
    copies_b = rims(1, count_b, t_b)
    for copy in copies_b:
        copy.start()
    o_copy.wait()
    m_copy.wait()
    sel = selector(owner_ref)

    for copy in copies_a:
        copy.wait()
    got = rim_added(count_a, t_a, r_next.at[0], r_prev.at[0], r_side.at[0], r_corner.at[0])
    for fl in range(4 * LEV):
        mean_ref[fl] = got[fl]
    for k in range(4):
        for lev in range(LEV):
            p, q = PAIRS[k]
            s_a[(k * LEV + lev) * 8 : (k * LEV + lev) * 8 + 8] = (
                got[(4 + k) * LEV + lev] - got[p * LEV + lev] * got[q * LEV + lev])
    src_a[...] = slots(2, sel, s_a, m_ref).reshape(n, 2, 256)
    own_a = hand_over(0, src_a, dst_a)

    for copy in copies_b:
        copy.wait()
    got = rim_added(count_b, t_b, r_next.at[1], r_prev.at[1], r_side.at[1], r_corner.at[1])
    for k in range(len(ROUND_B)):
        for lev in range(LEV):
            p, q = ROUND_B[k]
            s_b[(k * LEV + lev) * 8 : (k * LEV + lev) * 8 + 8] = (
                got[k * LEV + lev] - mean_ref[p * LEV + lev] * mean_ref[q * LEV + lev])
    src_b[...] = slots(3, sel, s_b, m_ref).reshape(n, 2, 384)
    own_b = hand_over(1, src_b, dst_b)

    rest = pl.ds(0, n - 1)
    own_a.wait()
    pltpu.make_async_copy(dst_a.at[rest], dst_a.at[rest], rsem.at[0]).wait()
    out_ref[:, 0:256] = dst_a[...].reshape(2 * n, 256)
    own_b.wait()
    pltpu.make_async_copy(dst_b.at[rest], dst_b.at[rest], rsem.at[1]).wait()
    out_ref[:, 256:640] = dst_b[...].reshape(2 * n, 384)
    pltpu.make_async_copy(src_a.at[rest], src_a.at[rest], ssem.at[0]).wait()
    pltpu.make_async_copy(src_b.at[rest], src_b.at[rest], ssem.at[1]).wait()


def per_device(fields, owner):
    n_gx, n_gy = lax.axis_size("gx"), lax.axis_size("gy")
    n = n_gx * n_gy
    taps = gauss_taps()
    g = [float(x) for x in taps]
    length = fields.shape[-1]
    weights = jnp.asarray(east_matrix(length, taps))
    blocks = jnp.asarray(block_matrix(), jnp.bfloat16)
    f32 = jnp.float32
    rows_a, rows_b = (len(r) * LEV * 8 + 2 * SIDE for r in (ROUND_A, ROUND_B))
    return pl.pallas_call(
        functools.partial(kernel, n_gx, n_gy, g),
        out_shape=jax.ShapeDtypeStruct((2 * n, 640), f32),
        in_specs=[pl.BlockSpec(memory_space=pltpu.HBM)] * 4,
        out_specs=pl.BlockSpec(memory_space=pltpu.VMEM),
        scratch_shapes=[
            pltpu.VMEM((length // 128, 4, LEV, 80, 128), f32),
            pltpu.VMEM((length // KC, KC, 256), f32),
            pltpu.VMEM((256, 256), jnp.bfloat16),
            pltpu.VMEM((1, 64), jnp.int32),
            pltpu.VMEM((rows_a, KC), f32),
            pltpu.VMEM((rows_b, KC), f32),
            pltpu.VMEM((rows_a, 256), f32),
            pltpu.VMEM((rows_b, 256), f32),
            pltpu.VMEM((4 * LEV, 8, 128), f32),
            pltpu.VMEM((128, 128), f32),
            pltpu.VMEM((256, 128), f32),
            pltpu.VMEM((n, 2, 256), f32),
            pltpu.VMEM((n, 2, 384), f32),
            pltpu.VMEM((n, 2, 256), f32),
            pltpu.VMEM((n, 2, 384), f32),
            pltpu.VMEM((2, 8, 128), f32),
            pltpu.VMEM((2, 8, 128), f32),
            pltpu.VMEM((2, SIDE, 128), f32),
            pltpu.VMEM((2, SIDE, 128), f32),
            pltpu.VMEM((2, 2, 8, 128), f32),
            pltpu.VMEM((2, 4, 8, 128), f32),
            pltpu.SemaphoreType.DMA((length // 128,)),
            pltpu.SemaphoreType.DMA((length // KC,)),
            pltpu.SemaphoreType.DMA,
            pltpu.SemaphoreType.DMA,
            pltpu.SemaphoreType.DMA((2,)),
            pltpu.SemaphoreType.DMA((2,)),
            pltpu.SemaphoreType.DMA((2, 8)),
            pltpu.SemaphoreType.DMA((2, 8)),
            pltpu.SemaphoreType.DMA((2,)),
        ],
        compiler_params=pltpu.CompilerParams(
            collective_id=0, has_side_effects=True, vmem_limit_bytes=24 << 20
        ),
    )(*(pltpu.with_memory_space_constraint(x, pltpu.HBM) for x in (fields, weights, blocks, owner.reshape(1, 64))))


def solution(mesh):
    placed = (P(None, None, "gy", "gx"), P(("gx", "gy"), None))
    return jax.shard_map(
        per_device, mesh=mesh, in_specs=placed, out_specs=P(("gx", "gy"), None), check_vma=False
    )
```

```python
import functools

import jax
import jax.numpy as jnp
import numpy as np
from jax import lax
from jax.experimental import pallas as pl
from jax.experimental.pallas import tpu as pltpu
from jax.sharding import PartitionSpec as P

MESH = pl.DeviceIdType.MESH
LOGICAL = pl.DeviceIdType.LOGICAL
BLK = 4
FIRST = 4
LEV = 4
RATIO = 10
TAPS = 21
SIGMA_CELLS = 2.8867513
PAIRS = ((0, 0), (0, 1), (0, 2), (0, 3), (1, 1), (1, 2), (1, 3), (2, 2), (2, 3), (3, 3))
ROUND_A = tuple((a, None) for a in range(4)) + PAIRS[:FIRST]
ROUND_B = PAIRS[FIRST:]
KC = 256
AHEAD = 2
ORDER = (0, 3, 1, 2)
LANE_LAST = 63


def gauss_taps():
    spread = np.arange(TAPS, dtype=np.float32) - np.float32(10.0)
    values = np.exp(-spread * spread / np.float32(2.0 * SIGMA_CELLS * SIGMA_CELLS)).astype(np.float32)
    return (values / values.sum(dtype=np.float32)).astype(np.float32)


def east_matrix(length, taps):
    coarse = length // RATIO
    w = np.zeros((length, 256), np.float32)
    cols = [(128, coarse), (128 + LANE_LAST, -1)]
    for lane in range(128):
        cols.append((lane, 4 * (lane % 32) + ORDER[lane // 32]))
    for lane, j in cols:
        for t in range(TAPS):
            x = RATIO * j - 5 + t
            if 0 <= x < length:
                w[x, lane] = taps[t]
    return w


def east_parts(w):
    parts = []
    for _ in range(3):
        parts.append(w.astype(jnp.bfloat16))
        w = w - parts[-1].astype(np.float32)
    hi, mid, lo = (p.reshape(-1, 1, KC, 256) for p in parts)
    return np.concatenate([hi, mid, lo], axis=1)


def block_matrix():
    m = np.zeros((256, 256), np.float32)
    for grp in range(4):
        for kl in range(8):
            for i in range(8):
                by, r = divmod(i, 4)
                m[grp * 64 + kl * 8 + i, by * 128 + kl * 16 + r * 4 + ORDER[grp]] = 1.0
    return m


def split3(x):
    hi = x.astype(jnp.bfloat16)
    rest = x - hi.astype(jnp.float32)
    mid = rest.astype(jnp.bfloat16)
    lo = (rest - mid.astype(jnp.float32)).astype(jnp.bfloat16)
    return hi, mid, lo


def east(x, w_ref):
    rows = x.shape[0]
    parts = jnp.concatenate(split3(x), axis=0)
    out = None
    for i in range(3):
        p = jnp.dot(parts[: (3 - i) * rows], w_ref[i], preferred_element_type=jnp.float32)
        for j in range(3 - i):
            v = p[j * rows : j * rows + rows]
            out = v if out is None else out + v
    return out


def side_rows(fields):
    return -(-len(fields) * LEV // 8) * 8


def places(fields):
    return [(lev * len(fields) + f,) * 2 for lev in range(LEV) for f in range(len(fields))]


def iota(shape, dim):
    return lax.broadcasted_iota(jnp.int32, shape, dim)


def north_parts(v, g):
    q5, q0 = g[5] * v[0], g[0] * v[5]
    a = q5 + g[10] * v[5] + g[9] * (v[4] + v[6]) + g[8] * (v[3] + v[7]) + g[7] * (v[2] + v[8]) + g[6] * (v[1] + v[9])
    b = q0 + g[1] * v[6] + g[2] * v[7] + g[3] * v[8] + g[4] * v[9]
    c = q5 + q0 + g[4] * v[1] + g[3] * v[2] + g[2] * v[3] + g[1] * v[4]
    return a, b, c


def north_chunk(fields, f_ref, kc, x_ref, g):
    row = iota((8, 128), 0)
    main, side = len(fields) * LEV * 8, side_rows(fields)
    used = sorted({a for pair in fields for a in pair if a is not None})

    def piece(lev, lt, lanes):
        x = {a: [f_ref[kc * (KC // 128) + lt, a, lev, pl.ds(o, 8, stride=RATIO), :] for o in range(RATIO)] for a in used}
        for f, (p, q) in enumerate(fields):
            v = x[p] if q is None else [x[p][o] * x[q][o] for o in range(RATIO)]
            a, b, c = north_parts(v, g)
            b = pltpu.roll(b, 1, 0)
            c = pltpu.roll(c, 7, 0)
            at = (lev * len(fields) + f) * 8
            x_ref[pl.ds(at, 8), lanes] = a + jnp.where(row == 0, 0.0, b) + jnp.where(row == 7, 0.0, c)
            up = main + lev * len(fields) + f
            x_ref[up : up + 1, lanes] = b[0:1]
            x_ref[up + side : up + side + 1, lanes] = c[7:8]

    for lev in range(LEV):
        for lt in range(KC // 128):
            piece(lev, lt, slice(lt * 128, lt * 128 + 128))


def selector(owner_ref):
    own = owner_ref[...].astype(jnp.float32)
    row = jnp.broadcast_to(jnp.concatenate([own, own], axis=1), (128, 128))
    col = row.T[:64]
    before = (col == row[:64]) & (iota((64, 128), 0) < (iota((64, 128), 1) & 63))
    rank = jnp.sum(before.astype(jnp.float32), axis=0, keepdims=True)
    slot = row[0:1] * 2.0 + rank
    where = iota((256, 128), 0).astype(jnp.float32)
    return (where == slot).astype(jnp.bfloat16)


def pack_rim(fields, t_ref, edge, corner):
    lane = iota((8, 128), 1)
    row = iota((8, 128), 0)
    keep = (lane == 0) | (lane == LANE_LAST)
    packed = jnp.zeros((8, 128), jnp.float32)
    for at, sl in places(fields):
        v = jnp.where(keep, t_ref[at * 8 : at * 8 + 8, 128:256], 0.0)
        packed = packed + (pltpu.roll(v, sl, 1) if sl else v)
    edge[...] = packed
    rows = len(fields) * LEV * 8 + 2 * side_rows(fields)
    turned = t_ref[rows - 128 : rows, 128:256].T
    corner[...] = jnp.where(row == 0, turned[0:1], turned[LANE_LAST : LANE_LAST + 1])


def rim_copies(n_gx, n_gy, gx, gy, fields, t_ref, edge, corner, r_next, r_prev, r_side, r_corner, hsend, hrecv):
    east, west = lax.rem(gx + 1, n_gx), lax.rem(gx + n_gx - 1, n_gx)
    up, down = lax.rem(gy + 1, n_gy), lax.rem(gy + n_gy - 1, n_gy)
    main, n_side = len(fields) * LEV * 8, side_rows(fields)
    moves = (
        (t_ref.at[main : main + n_side, 0:128], r_next.at[:n_side], (gx, up)),
        (t_ref.at[main + n_side : main + 2 * n_side, 0:128], r_prev.at[:n_side], (gx, down)),
        (edge, r_side.at[0], (east, gy)),
        (edge, r_side.at[1], (west, gy)),
        (corner, r_corner.at[0], (east, up)),
        (corner, r_corner.at[1], (east, down)),
        (corner, r_corner.at[2], (west, up)),
        (corner, r_corner.at[3], (west, down)),
    )
    return [
        pltpu.make_async_remote_copy(s, d, hsend.at[i], hrecv.at[i], device_id=to, device_id_type=MESH)
        for i, (s, d, to) in enumerate(moves)
    ]


def rim_added(fields, t_ref, r_next, r_prev, r_side, r_corner):
    lane = iota((8, 128), 1)
    row = iota((8, 128), 0)
    keep = (lane == 0) | (lane == LANE_LAST)
    side = jnp.where(lane < LANE_LAST, r_side[0], r_side[1])
    n_side = side_rows(fields)
    first = lane < n_side
    secnd = (lane >= LANE_LAST) & (lane < LANE_LAST + n_side)
    corners = (
        (first, 0, 0, 2 * n_side % 128),
        (first, 7, 0, n_side),
        (secnd, 0, 1, (LANE_LAST + 2 * n_side) % 128),
        (secnd, 7, 1, (LANE_LAST + n_side) % 128),
    )
    for i, (lanes, at, got, turn) in enumerate(corners):
        v = jnp.broadcast_to(r_corner[i, got : got + 1], (8, 128))
        side = side + jnp.where(lanes & (row == at), pltpu.roll(v, turn, 1), 0.0)
    out = []
    for at, sl in places(fields):
        v = t_ref[at * 8 : at * 8 + 8, 0:128]
        v = v + jnp.where(row == 0, r_next[sl : sl + 1], 0.0) + jnp.where(row == 7, r_prev[sl : sl + 1], 0.0)
        out.append(v + jnp.where(keep, pltpu.roll(side, 128 - sl, 1) if sl else side, 0.0))
    return out


def slots(groups, sel, s_ref, m_ref):
    half = iota((32, 128), 1) < 64
    tiles = []
    for tt in range((groups + 1) // 2):
        st = s_ref[tt * 128 : tt * 128 + 128].T
        rt = pltpu.roll(st, 64, 1)
        left = [st[i * 32 : i * 32 + 32] for i in range(4)]
        right = [rt[i * 32 : i * 32 + 32] for i in range(4)]
        tiles.append((jnp.where(half, left[0], right[1]), jnp.where(half, left[2], right[3])))
        tiles.append((jnp.where(half, right[0], left[1]), jnp.where(half, right[2], left[3])))
    tiles = tiles[:groups]
    lhs = jnp.concatenate([jnp.concatenate([a, b], axis=1) for a, b in tiles], axis=0)
    lhs = jnp.concatenate(split3(lhs), axis=0)
    o = jnp.dot(lhs, m_ref[...], preferred_element_type=jnp.float32).astype(jnp.bfloat16)
    pay = []
    for part in range(3):
        for by in range(2):
            at = part * groups * 32
            pay.append(jnp.concatenate(
                [o[at + gg * 32 : at + gg * 32 + 32, by * 128 : by * 128 + 128] for gg in range(groups)], axis=1))
    out = jnp.dot(sel, jnp.concatenate(pay[0:4], axis=0), preferred_element_type=jnp.float32)
    return out + jnp.dot(sel[:, :64], jnp.concatenate(pay[4:6], axis=0), preferred_element_type=jnp.float32)


def kernel(n_gx, n_gy, g, f_hbm, w_hbm, m_hbm, o_hbm, out_ref, f_ref, w_ref, m_ref, owner_ref, x_a, x_b, t_a, t_b,
           mean_ref, s_a, s_b, src_a, src_b, dst_a, dst_b, edge, corner, r_next, r_prev, r_side, r_corner,
           fsem, wsem, msem, osem, ssem, rsem, hsend, hrecv, lsem):
    n = n_gx * n_gy
    gx, gy = lax.axis_index("gx"), lax.axis_index("gy")
    me = gx * n_gy + gy
    steps = w_ref.shape[0]
    per = KC // 128
    wide = FIRST * 64

    def f_copy(lt):
        return pltpu.make_async_copy(f_hbm.at[:, :, :, pl.ds(pl.multiple_of(lt * 128, 128), 128)], f_ref.at[lt], fsem.at[lt])

    def w_copy(kc):
        return pltpu.make_async_copy(w_hbm.at[kc], w_ref.at[kc], wsem.at[kc])

    def fetch(kc):
        for lt in range(per):
            f_copy(kc * per + lt).start()
        w_copy(kc).start()

    for kc in range(AHEAD):
        fetch(kc)
    m_copy = pltpu.make_async_copy(m_hbm, m_ref, msem)
    m_copy.start()
    o_copy = pltpu.make_async_copy(o_hbm, owner_ref, osem)
    o_copy.start()

    barrier = pltpu.get_barrier_semaphore()

    def greet(k, carry):
        d = lax.rem(me + k, n)
        pl.semaphore_signal(barrier, inc=1, device_id=d, device_id_type=LOGICAL)
        return carry

    lax.fori_loop(1, n, greet, 0, unroll=8)

    def local(fields, x_ref, t_ref, fresh):
        main = len(fields) * LEV * 8
        n_side = side_rows(fields)
        x_ref[main : main + 2 * n_side] = jnp.zeros((2 * n_side, KC), jnp.float32)
        t_ref[...] = jnp.zeros_like(t_ref)

        def chunk(kc, carry):
            if fresh:
                for lt in range(per):
                    f_copy(kc * per + lt).wait()
                pl.when(kc + AHEAD < steps)(lambda: fetch(kc + AHEAD))
            north_chunk(fields, f_ref, kc, x_ref, g)
            if fresh:
                w_copy(kc).wait()
            t_ref[...] += east(x_ref[...], w_ref.at[kc])
            return carry

        lax.fori_loop(0, steps, chunk, 0)

    def rims(i, fields, t_ref):
        bufs = (edge, corner, r_next, r_prev, r_side, r_corner, hsend, hrecv)
        return rim_copies(n_gx, n_gy, gx, gy, fields, t_ref, *(b.at[i] for b in bufs))

    def hand_over(i, src, dst):
        own = pltpu.make_async_copy(src.at[me], dst.at[me], lsem.at[i])
        own.start()

        def send(k, carry):
            d = lax.rem(me + k, n)
            pltpu.make_async_remote_copy(
                src.at[d], dst.at[me], ssem.at[i], rsem.at[i],
                device_id=d, device_id_type=LOGICAL,
            ).start()
            return carry

        lax.fori_loop(1, n, send, 0, unroll=8)
        return own

    local(ROUND_A, x_a, t_a, True)
    pack_rim(ROUND_A, t_a, edge.at[0], corner.at[0])
    pl.semaphore_wait(barrier, n - 1)
    copies_a = rims(0, ROUND_A, t_a)
    for copy in copies_a:
        copy.start()
    local(ROUND_B, x_b, t_b, False)
    pack_rim(ROUND_B, t_b, edge.at[1], corner.at[1])
    copies_b = rims(1, ROUND_B, t_b)
    for copy in copies_b:
        copy.start()
    o_copy.wait()
    m_copy.wait()
    sel = selector(owner_ref)

    for copy in copies_a:
        copy.wait()
    got = rim_added(ROUND_A, t_a, r_next.at[0], r_prev.at[0], r_side.at[0], r_corner.at[0])
    for lev in range(LEV):
        for a in range(4):
            mean_ref[lev * 4 + a] = got[lev * len(ROUND_A) + a]
    for k in range(FIRST):
        for lev in range(LEV):
            p, q = PAIRS[k]
            s_a[(k * LEV + lev) * 8 : (k * LEV + lev) * 8 + 8] = (
                got[lev * len(ROUND_A) + 4 + k] - got[lev * len(ROUND_A) + p] * got[lev * len(ROUND_A) + q])
    src_a[...] = slots(FIRST // 2, sel, s_a, m_ref).reshape(n, 2, wide)
    own_a = hand_over(0, src_a, dst_a)

    for copy in copies_b:
        copy.wait()
    got = rim_added(ROUND_B, t_b, r_next.at[1], r_prev.at[1], r_side.at[1], r_corner.at[1])
    for k in range(len(ROUND_B)):
        for lev in range(LEV):
            p, q = ROUND_B[k]
            s_b[(k * LEV + lev) * 8 : (k * LEV + lev) * 8 + 8] = (
                got[lev * len(ROUND_B) + k] - mean_ref[lev * 4 + p] * mean_ref[lev * 4 + q])
    src_b[...] = slots(len(ROUND_B) // 2, sel, s_b, m_ref).reshape(n, 2, 640 - wide)
    own_b = hand_over(1, src_b, dst_b)

    rest = pl.ds(0, n - 1)
    own_a.wait()
    pltpu.make_async_copy(dst_a.at[rest], dst_a.at[rest], rsem.at[0]).wait()
    out_ref[:, :wide] = dst_a[...].reshape(2 * n, wide)
    own_b.wait()
    pltpu.make_async_copy(dst_b.at[rest], dst_b.at[rest], rsem.at[1]).wait()
    out_ref[:, wide:] = dst_b[...].reshape(2 * n, 640 - wide)
    pltpu.make_async_copy(src_a.at[rest], src_a.at[rest], ssem.at[0]).wait()
    pltpu.make_async_copy(src_b.at[rest], src_b.at[rest], ssem.at[1]).wait()


def per_device(fields, owner):
    n_gx, n_gy = lax.axis_size("gx"), lax.axis_size("gy")
    n = n_gx * n_gy
    taps = gauss_taps()
    g = [float(x) for x in taps]
    length = fields.shape[-1]
    weights = jnp.asarray(east_parts(east_matrix(length, taps)))
    blocks = jnp.asarray(block_matrix(), jnp.bfloat16)
    f32 = jnp.float32
    wide = FIRST * 64
    side = side_rows(ROUND_A)
    rows_a, rows_b = (len(r) * LEV * 8 + 2 * side_rows(r) for r in (ROUND_A, ROUND_B))
    return pl.pallas_call(
        functools.partial(kernel, n_gx, n_gy, g),
        out_shape=jax.ShapeDtypeStruct((2 * n, 640), f32),
        in_specs=[pl.BlockSpec(memory_space=pltpu.HBM)] * 4,
        out_specs=pl.BlockSpec(memory_space=pltpu.VMEM),
        scratch_shapes=[
            pltpu.VMEM((length // 128, 4, LEV, 80, 128), f32),
            pltpu.VMEM((length // KC, 3, KC, 256), jnp.bfloat16),
            pltpu.VMEM((256, 256), jnp.bfloat16),
            pltpu.VMEM((1, 64), jnp.int32),
            pltpu.VMEM((rows_a, KC), f32),
            pltpu.VMEM((rows_b, KC), f32),
            pltpu.VMEM((rows_a, 256), f32),
            pltpu.VMEM((rows_b, 256), f32),
            pltpu.VMEM((4 * LEV, 8, 128), f32),
            pltpu.VMEM((-(-FIRST // 4) * 128, 128), f32),
            pltpu.VMEM((-(-len(ROUND_B) // 4) * 128, 128), f32),
            pltpu.VMEM((n, 2, wide), f32),
            pltpu.VMEM((n, 2, 640 - wide), f32),
            pltpu.VMEM((n, 2, wide), f32),
            pltpu.VMEM((n, 2, 640 - wide), f32),
            pltpu.VMEM((2, 8, 128), f32),
            pltpu.VMEM((2, 8, 128), f32),
            pltpu.VMEM((2, side, 128), f32),
            pltpu.VMEM((2, side, 128), f32),
            pltpu.VMEM((2, 2, 8, 128), f32),
            pltpu.VMEM((2, 4, 8, 128), f32),
            pltpu.SemaphoreType.DMA((length // 128,)),
            pltpu.SemaphoreType.DMA((length // KC,)),
            pltpu.SemaphoreType.DMA,
            pltpu.SemaphoreType.DMA,
            pltpu.SemaphoreType.DMA((2,)),
            pltpu.SemaphoreType.DMA((2,)),
            pltpu.SemaphoreType.DMA((2, 8)),
            pltpu.SemaphoreType.DMA((2, 8)),
            pltpu.SemaphoreType.DMA((2,)),
        ],
        compiler_params=pltpu.CompilerParams(
            collective_id=0, has_side_effects=True, vmem_limit_bytes=24 << 20
        ),
    )(*(pltpu.with_memory_space_constraint(x, pltpu.HBM) for x in (fields, weights, blocks, owner.reshape(1, 64))))


def solution(mesh):
    placed = (P(None, None, "gy", "gx"), P(("gx", "gy"), None))
    return jax.shard_map(
        per_device, mesh=mesh, in_specs=placed, out_specs=P(("gx", "gy"), None), check_vma=False
    )
```

```python
import functools

import jax
import jax.numpy as jnp
import numpy as np
from jax import lax
from jax.experimental import pallas as pl
from jax.experimental.pallas import tpu as pltpu
from jax.sharding import PartitionSpec as P

MESH = pl.DeviceIdType.MESH
LOGICAL = pl.DeviceIdType.LOGICAL
BLK = 4
FIRST = 4
LEV = 4
RATIO = 10
TAPS = 21
SIGMA_CELLS = 2.8867513
PAIRS = ((0, 0), (0, 1), (0, 2), (0, 3), (1, 1), (1, 2), (1, 3), (2, 2), (2, 3), (3, 3))
ROUND_A = tuple((a, None) for a in range(4)) + PAIRS[:FIRST]
ROUND_B = PAIRS[FIRST:]
KC = 256
AHEAD = 3
ORDER = (0, 3, 1, 2)
LANE_LAST = 63


def gauss_taps():
    spread = np.arange(TAPS, dtype=np.float32) - np.float32(10.0)
    values = np.exp(-spread * spread / np.float32(2.0 * SIGMA_CELLS * SIGMA_CELLS)).astype(np.float32)
    return (values / values.sum(dtype=np.float32)).astype(np.float32)


def east_matrix(length, taps):
    coarse = length // RATIO
    w = np.zeros((length, 256), np.float32)
    cols = [(128, coarse), (128 + LANE_LAST, -1)]
    for lane in range(128):
        cols.append((lane, 4 * (lane % 32) + ORDER[lane // 32]))
    for lane, j in cols:
        for t in range(TAPS):
            x = RATIO * j - 5 + t
            if 0 <= x < length:
                w[x, lane] = taps[t]
    return w


def east_parts(w):
    parts = []
    for _ in range(3):
        parts.append(w.astype(jnp.bfloat16))
        w = w - parts[-1].astype(np.float32)
    hi, mid, lo = (p.reshape(-1, 1, KC, 256) for p in parts)
    rim = hi[..., 128:] + np.roll(mid[..., 128:], 1, -1) + np.roll(lo[..., 128:], 2, -1)
    return np.concatenate(
        [np.concatenate([hi[..., :128], mid[..., :128]], -1), np.concatenate([lo[..., :128], rim], -1)], axis=1)


def block_matrix():
    m = np.zeros((256, 256), np.float32)
    for grp in range(4):
        for kl in range(8):
            for i in range(8):
                by, r = divmod(i, 4)
                m[grp * 64 + kl * 8 + i, by * 128 + kl * 16 + r * 4 + ORDER[grp]] = 1.0
    return m


def split3(x):
    hi = x.astype(jnp.bfloat16)
    rest = x - hi.astype(jnp.float32)
    mid = rest.astype(jnp.bfloat16)
    lo = (rest - mid.astype(jnp.float32)).astype(jnp.bfloat16)
    return hi, mid, lo


def east(x, w_ref, rim):
    rows = x.shape[0]
    parts = jnp.concatenate(split3(x), axis=0)
    p = jnp.dot(parts, w_ref[0], preferred_element_type=jnp.float32)
    q = jnp.dot(parts if rim else parts[:rows], w_ref[1], preferred_element_type=jnp.float32)
    out = q[:rows, :128] + p[2 * rows :, :128] + p[rows : 2 * rows, 128:]
    out = out + (p[rows : 2 * rows, :128] + p[:rows, 128:])
    out = out + p[:rows, :128]
    if not rim:
        return out, None
    return out, q[2 * rows :, 128:] + q[rows : 2 * rows, 128:] + q[:rows, 128:]


def side_rows(fields):
    return -(-len(fields) * LEV // 8) * 8


def places(fields):
    return [(lev * len(fields) + f,) * 2 for lev in range(LEV) for f in range(len(fields))]


def iota(shape, dim):
    return lax.broadcasted_iota(jnp.int32, shape, dim)


def north_parts(v, g):
    q5, q0 = g[5] * v[0], g[0] * v[5]
    a = q5 + g[10] * v[5] + g[9] * (v[4] + v[6]) + g[8] * (v[3] + v[7]) + g[7] * (v[2] + v[8]) + g[6] * (v[1] + v[9])
    b = q0 + g[1] * v[6] + g[2] * v[7] + g[3] * v[8] + g[4] * v[9]
    c = q5 + q0 + g[4] * v[1] + g[3] * v[2] + g[2] * v[3] + g[1] * v[4]
    return a, b, c


def north_chunk(fields, f_ref, kc, x_ref, g):
    row = iota((8, 128), 0)
    main, side = len(fields) * LEV * 8, side_rows(fields)
    used = sorted({a for pair in fields for a in pair if a is not None})

    def piece(lev, lt, lanes):
        x = {a: [f_ref[kc * (KC // 128) + lt, a, lev, pl.ds(o, 8, stride=RATIO), :] for o in range(RATIO)] for a in used}
        for f, (p, q) in enumerate(fields):
            v = x[p] if q is None else [x[p][o] * x[q][o] for o in range(RATIO)]
            a, b, c = north_parts(v, g)
            b = pltpu.roll(b, 1, 0)
            c = pltpu.roll(c, 7, 0)
            at = (lev * len(fields) + f) * 8
            x_ref[pl.ds(at, 8), lanes] = a + jnp.where(row == 0, 0.0, b) + jnp.where(row == 7, 0.0, c)
            up = main + lev * len(fields) + f
            x_ref[up : up + 1, lanes] = b[0:1]
            x_ref[up + side : up + side + 1, lanes] = c[7:8]

    for lev in range(LEV):
        for lt in range(KC // 128):
            piece(lev, lt, slice(lt * 128, lt * 128 + 128))


def selector(owner_ref):
    own = owner_ref[...].astype(jnp.float32)
    row = jnp.broadcast_to(jnp.concatenate([own, own], axis=1), (128, 128))
    col = row.T[:64]
    before = (col == row[:64]) & (iota((64, 128), 0) < (iota((64, 128), 1) & 63))
    rank = jnp.sum(before.astype(jnp.float32), axis=0, keepdims=True)
    slot = row[0:1] * 2.0 + rank
    where = iota((256, 128), 0).astype(jnp.float32)
    sel = (where == slot).astype(jnp.bfloat16)
    return jnp.concatenate([sel, sel[:, :64]], axis=1)


def pack_rim(fields, t_ref, edge, corner):
    lane = iota((8, 128), 1)
    row = iota((8, 128), 0)
    keep = (lane == 0) | (lane == LANE_LAST)
    packed = jnp.zeros((8, 128), jnp.float32)
    for at, sl in places(fields):
        v = jnp.where(keep, t_ref[at * 8 : at * 8 + 8, 128:256], 0.0)
        packed = packed + (pltpu.roll(v, sl, 1) if sl else v)
    edge[...] = packed
    rows = len(fields) * LEV * 8 + 2 * side_rows(fields)
    turned = t_ref[rows - 128 : rows, 128:256].T
    corner[...] = jnp.where(row == 0, turned[0:1], turned[LANE_LAST : LANE_LAST + 1])


def rim_copies(n_gx, n_gy, gx, gy, fields, t_ref, edge, corner, r_next, r_prev, r_side, r_corner, hsend, hrecv):
    east, west = lax.rem(gx + 1, n_gx), lax.rem(gx + n_gx - 1, n_gx)
    up, down = lax.rem(gy + 1, n_gy), lax.rem(gy + n_gy - 1, n_gy)
    main, n_side = len(fields) * LEV * 8, side_rows(fields)
    moves = (
        (t_ref.at[main : main + n_side, 0:128], r_next.at[:n_side], (gx, up)),
        (t_ref.at[main + n_side : main + 2 * n_side, 0:128], r_prev.at[:n_side], (gx, down)),
        (edge, r_side.at[0], (east, gy)),
        (edge, r_side.at[1], (west, gy)),
        (corner, r_corner.at[0], (east, up)),
        (corner, r_corner.at[1], (east, down)),
        (corner, r_corner.at[2], (west, up)),
        (corner, r_corner.at[3], (west, down)),
    )
    return [
        pltpu.make_async_remote_copy(s, d, hsend.at[i], hrecv.at[i], device_id=to, device_id_type=MESH)
        for i, (s, d, to) in enumerate(moves)
    ]


def rim_added(fields, t_ref, r_next, r_prev, r_side, r_corner):
    lane = iota((8, 128), 1)
    row = iota((8, 128), 0)
    keep = (lane == 0) | (lane == LANE_LAST)
    side = jnp.where(lane < LANE_LAST, r_side[0], r_side[1])
    n_side = side_rows(fields)
    first = lane < n_side
    secnd = (lane >= LANE_LAST) & (lane < LANE_LAST + n_side)
    corners = (
        (first, 0, 0, 2 * n_side % 128),
        (first, 7, 0, n_side),
        (secnd, 0, 1, (LANE_LAST + 2 * n_side) % 128),
        (secnd, 7, 1, (LANE_LAST + n_side) % 128),
    )
    for i, (lanes, at, got, turn) in enumerate(corners):
        v = jnp.broadcast_to(r_corner[i, got : got + 1], (8, 128))
        side = side + jnp.where(lanes & (row == at), pltpu.roll(v, turn, 1), 0.0)
    out = []
    for at, sl in places(fields):
        v = t_ref[at * 8 : at * 8 + 8, 0:128]
        v = v + jnp.where(row == 0, r_next[sl : sl + 1], 0.0) + jnp.where(row == 7, r_prev[sl : sl + 1], 0.0)
        out.append(v + jnp.where(keep, pltpu.roll(side, 128 - sl, 1) if sl else side, 0.0))
    return out


def slots(groups, sel, s_ref, m_ref):
    half = iota((32, 128), 1) < 64
    tiles = []
    for tt in range((groups + 1) // 2):
        st = s_ref[tt * 128 : tt * 128 + 128].T
        rt = pltpu.roll(st, 64, 1)
        left = [st[i * 32 : i * 32 + 32] for i in range(4)]
        right = [rt[i * 32 : i * 32 + 32] for i in range(4)]
        tiles.append((jnp.where(half, left[0], right[1]), jnp.where(half, left[2], right[3])))
        tiles.append((jnp.where(half, right[0], left[1]), jnp.where(half, right[2], left[3])))
    tiles = tiles[:groups]
    lhs = jnp.concatenate([jnp.concatenate([a, b], axis=1) for a, b in tiles], axis=0)
    lhs = jnp.concatenate(split3(lhs), axis=0)
    o = jnp.dot(lhs, m_ref[...], preferred_element_type=jnp.float32).astype(jnp.bfloat16)
    pay = []
    for part in range(3):
        for by in range(2):
            at = part * groups * 32
            pay.append(jnp.concatenate(
                [o[at + gg * 32 : at + gg * 32 + 32, by * 128 : by * 128 + 128] for gg in range(groups)], axis=1))
    return jnp.dot(sel, jnp.concatenate(pay, axis=0), preferred_element_type=jnp.float32)


def kernel(n_gx, n_gy, g, f_hbm, w_hbm, m_hbm, o_hbm, out_ref, f_ref, w_ref, m_ref, owner_ref, x_a, x_b, x_b1, t_a, t_b,
           mean_ref, s_a, s_b, src_a, src_b, dst_a, dst_b, edge, corner, r_next, r_prev, r_side, r_corner,
           fsem, wsem, msem, osem, ssem, rsem, hsend, hrecv, lsem):
    n = n_gx * n_gy
    gx, gy = lax.axis_index("gx"), lax.axis_index("gy")
    me = gx * n_gy + gy
    steps = w_ref.shape[0]
    per = KC // 128
    wide = FIRST * 64

    def f_copy(lt):
        return pltpu.make_async_copy(f_hbm.at[:, :, :, pl.ds(pl.multiple_of(lt * 128, 128), 128)], f_ref.at[lt], fsem.at[lt])

    def w_copy(kc):
        return pltpu.make_async_copy(w_hbm.at[kc], w_ref.at[kc], wsem.at[kc])

    def fetch(kc):
        for lt in range(per):
            f_copy(kc * per + lt).start()
        w_copy(kc).start()

    for kc in range(AHEAD):
        fetch(kc)
    m_copy = pltpu.make_async_copy(m_hbm, m_ref, msem)
    m_copy.start()
    o_copy = pltpu.make_async_copy(o_hbm, owner_ref, osem)
    o_copy.start()

    barrier = pltpu.get_barrier_semaphore()

    def greet(k, carry):
        d = lax.rem(me + k, n)
        pl.semaphore_signal(barrier, inc=1, device_id=d, device_id_type=LOGICAL)
        return carry

    lax.fori_loop(1, n, greet, 0, unroll=8)

    def local(fields, x_ref, t_ref, fresh, x_other=None):
        main = len(fields) * LEV * 8
        n_side = side_rows(fields)
        for ref in (x_ref, x_other):
            if ref is not None:
                ref[main : main + 2 * n_side] = jnp.zeros((2 * n_side, KC), jnp.float32)
        t_ref[...] = jnp.zeros_like(t_ref)

        def add(x, kc, rim):
            part, side = east(x[...], w_ref.at[kc], rim)
            t_ref[:, :128] += part
            if rim:
                t_ref[:, 128:] += side

        def chunk(kc, carry):
            for lt in range(per):
                f_copy(kc * per + lt).wait()
            pl.when(kc + AHEAD < steps)(lambda: fetch(kc + AHEAD))
            north_chunk(fields, f_ref, kc, x_ref, g)
            w_copy(kc).wait()
            rim = (kc == 0) | (kc == steps - 1)
            pl.when(rim)(lambda: add(x_ref, kc, True))
            pl.when(jnp.logical_not(rim))(lambda: add(x_ref, kc, False))
            return carry

        if fresh:
            lax.fori_loop(0, steps, chunk, 0)
        else:
            bufs = (x_ref, x_other)
            for kc in range(steps):
                north_chunk(fields, f_ref, kc, bufs[kc % 2], g)
                if kc:
                    add(bufs[(kc - 1) % 2], kc - 1, kc == 1)
            add(bufs[(steps - 1) % 2], steps - 1, True)
        side = t_ref[:, 128:]
        t_ref[:, 128:] = side + pltpu.roll(side, 127, 1) + pltpu.roll(side, 126, 1)

    def rims(i, fields, t_ref):
        bufs = (edge, corner, r_next, r_prev, r_side, r_corner, hsend, hrecv)
        return rim_copies(n_gx, n_gy, gx, gy, fields, t_ref, *(b.at[i] for b in bufs))

    def hand_over(i, src, dst):
        own = pltpu.make_async_copy(src.at[me], dst.at[me], lsem.at[i])
        own.start()

        def send(k, carry):
            d = lax.rem(me + lax.rem(k, 4) * (n // 4) + lax.rem(k // 4, 4) * (n // 16) + k // 16, n)
            pltpu.make_async_remote_copy(
                src.at[d], dst.at[me], ssem.at[i], rsem.at[i],
                device_id=d, device_id_type=LOGICAL,
            ).start()
            return carry

        lax.fori_loop(1, n, send, 0, unroll=8)
        return own

    local(ROUND_A, x_a, t_a, True)
    pack_rim(ROUND_A, t_a, edge.at[0], corner.at[0])
    pl.semaphore_wait(barrier, n - 1)
    copies_a = rims(0, ROUND_A, t_a)
    for copy in copies_a:
        copy.start()
    local(ROUND_B, x_b, t_b, False, x_b1)
    pack_rim(ROUND_B, t_b, edge.at[1], corner.at[1])
    copies_b = rims(1, ROUND_B, t_b)
    for copy in copies_b:
        copy.start()
    o_copy.wait()
    m_copy.wait()
    sel = selector(owner_ref)

    for copy in copies_a:
        copy.wait()
    got = rim_added(ROUND_A, t_a, r_next.at[0], r_prev.at[0], r_side.at[0], r_corner.at[0])
    for lev in range(LEV):
        for a in range(4):
            mean_ref[lev * 4 + a] = got[lev * len(ROUND_A) + a]
    for k in range(FIRST):
        for lev in range(LEV):
            p, q = PAIRS[k]
            s_a[(k * LEV + lev) * 8 : (k * LEV + lev) * 8 + 8] = (
                got[lev * len(ROUND_A) + 4 + k] - got[lev * len(ROUND_A) + p] * got[lev * len(ROUND_A) + q])
    src_a[...] = slots(FIRST // 2, sel, s_a, m_ref).reshape(n, 2, wide)
    own_a = hand_over(0, src_a, dst_a)

    for copy in copies_b:
        copy.wait()
    got = rim_added(ROUND_B, t_b, r_next.at[1], r_prev.at[1], r_side.at[1], r_corner.at[1])
    for k in range(len(ROUND_B)):
        for lev in range(LEV):
            p, q = ROUND_B[k]
            s_b[(k * LEV + lev) * 8 : (k * LEV + lev) * 8 + 8] = (
                got[lev * len(ROUND_B) + k] - mean_ref[lev * 4 + p] * mean_ref[lev * 4 + q])
    src_b[...] = slots(len(ROUND_B) // 2, sel, s_b, m_ref).reshape(n, 2, 640 - wide)
    own_b = hand_over(1, src_b, dst_b)

    rest = pl.ds(0, n - 1)
    own_a.wait()
    pltpu.make_async_copy(dst_a.at[rest], dst_a.at[rest], rsem.at[0]).wait()
    out_ref[:, :wide] = dst_a[...].reshape(2 * n, wide)
    own_b.wait()
    pltpu.make_async_copy(dst_b.at[rest], dst_b.at[rest], rsem.at[1]).wait()
    out_ref[:, wide:] = dst_b[...].reshape(2 * n, 640 - wide)
    pltpu.make_async_copy(src_a.at[rest], src_a.at[rest], ssem.at[0]).wait()
    pltpu.make_async_copy(src_b.at[rest], src_b.at[rest], ssem.at[1]).wait()


def per_device(fields, owner):
    n_gx, n_gy = lax.axis_size("gx"), lax.axis_size("gy")
    n = n_gx * n_gy
    taps = gauss_taps()
    g = [float(x) for x in taps]
    length = fields.shape[-1]
    weights = jnp.asarray(east_parts(east_matrix(length, taps)))
    blocks = jnp.asarray(block_matrix(), jnp.bfloat16)
    f32 = jnp.float32
    wide = FIRST * 64
    side = side_rows(ROUND_A)
    rows_a, rows_b = (len(r) * LEV * 8 + 2 * side_rows(r) for r in (ROUND_A, ROUND_B))
    return pl.pallas_call(
        functools.partial(kernel, n_gx, n_gy, g),
        out_shape=jax.ShapeDtypeStruct((2 * n, 640), f32),
        in_specs=[pl.BlockSpec(memory_space=pltpu.HBM)] * 4,
        out_specs=pl.BlockSpec(memory_space=pltpu.VMEM),
        scratch_shapes=[
            pltpu.VMEM((length // 128, 4, LEV, 80, 128), f32),
            pltpu.VMEM((length // KC, 2, KC, 256), jnp.bfloat16),
            pltpu.VMEM((256, 256), jnp.bfloat16),
            pltpu.VMEM((1, 64), jnp.int32),
            pltpu.VMEM((rows_a, KC), f32),
            pltpu.VMEM((rows_b, KC), f32),
            pltpu.VMEM((rows_b, KC), f32),
            pltpu.VMEM((rows_a, 256), f32),
            pltpu.VMEM((rows_b, 256), f32),
            pltpu.VMEM((4 * LEV, 8, 128), f32),
            pltpu.VMEM((-(-FIRST // 4) * 128, 128), f32),
            pltpu.VMEM((-(-len(ROUND_B) // 4) * 128, 128), f32),
            pltpu.VMEM((n, 2, wide), f32),
            pltpu.VMEM((n, 2, 640 - wide), f32),
            pltpu.VMEM((n, 2, wide), f32),
            pltpu.VMEM((n, 2, 640 - wide), f32),
            pltpu.VMEM((2, 8, 128), f32),
            pltpu.VMEM((2, 8, 128), f32),
            pltpu.VMEM((2, side, 128), f32),
            pltpu.VMEM((2, side, 128), f32),
            pltpu.VMEM((2, 2, 8, 128), f32),
            pltpu.VMEM((2, 4, 8, 128), f32),
            pltpu.SemaphoreType.DMA((length // 128,)),
            pltpu.SemaphoreType.DMA((length // KC,)),
            pltpu.SemaphoreType.DMA,
            pltpu.SemaphoreType.DMA,
            pltpu.SemaphoreType.DMA((2,)),
            pltpu.SemaphoreType.DMA((2,)),
            pltpu.SemaphoreType.DMA((2, 8)),
            pltpu.SemaphoreType.DMA((2, 8)),
            pltpu.SemaphoreType.DMA((2,)),
        ],
        compiler_params=pltpu.CompilerParams(
            collective_id=0, has_side_effects=True, vmem_limit_bytes=24 << 20
        ),
    )(*(pltpu.with_memory_space_constraint(x, pltpu.HBM) for x in (fields, weights, blocks, owner.reshape(1, 64))))


def solution(mesh):
    placed = (P(None, None, "gy", "gx"), P(("gx", "gy"), None))
    return jax.shard_map(
        per_device, mesh=mesh, in_specs=placed, out_specs=P(("gx", "gy"), None), check_vma=False
    )
```

```python
import functools

import jax
import jax.numpy as jnp
import numpy as np
from jax import lax
from jax.experimental import pallas as pl
from jax.experimental.pallas import tpu as pltpu
from jax.sharding import PartitionSpec as P

MESH = pl.DeviceIdType.MESH
LOGICAL = pl.DeviceIdType.LOGICAL
BLK = 4
FIRST = 4
LEV = 4
RATIO = 10
TAPS = 21
SIGMA_CELLS = 2.8867513
PAIRS = ((0, 0), (0, 1), (0, 2), (0, 3), (1, 1), (1, 2), (1, 3), (2, 2), (2, 3), (3, 3))
ROUND_A = tuple((a, None) for a in range(4)) + PAIRS[:FIRST]
ROUND_B = PAIRS[FIRST:]
KC = 256
AHEAD = 3
ORDER = (0, 3, 1, 2)
LANE_LAST = 63


def gauss_taps():
    spread = np.arange(TAPS, dtype=np.float32) - np.float32(10.0)
    values = np.exp(-spread * spread / np.float32(2.0 * SIGMA_CELLS * SIGMA_CELLS)).astype(np.float32)
    return (values / values.sum(dtype=np.float32)).astype(np.float32)


def east_matrix(length, taps):
    coarse = length // RATIO
    w = np.zeros((length, 256), np.float32)
    cols = [(128, coarse), (128 + LANE_LAST, -1)]
    for lane in range(128):
        cols.append((lane, 4 * (lane % 32) + ORDER[lane // 32]))
    for lane, j in cols:
        for t in range(TAPS):
            x = RATIO * j - 5 + t
            if 0 <= x < length:
                w[x, lane] = taps[t]
    return w


def east_parts(w):
    parts = []
    for _ in range(3):
        parts.append(w.astype(jnp.bfloat16))
        w = w - parts[-1].astype(np.float32)
    hi, mid, lo = (p.reshape(-1, 1, KC, 256) for p in parts)
    rim = hi[..., 128:] + np.roll(mid[..., 128:], 1, -1) + np.roll(lo[..., 128:], 2, -1)
    return np.concatenate(
        [np.concatenate([hi[..., :128], mid[..., :128]], -1), np.concatenate([lo[..., :128], rim], -1)], axis=1)


def block_matrix():
    m = np.zeros((256, 256), np.float32)
    for grp in range(4):
        for kl in range(8):
            for i in range(8):
                by, r = divmod(i, 4)
                m[grp * 64 + kl * 8 + i, by * 128 + kl * 16 + r * 4 + ORDER[grp]] = 1.0
    return m


def split3(x):
    hi = x.astype(jnp.bfloat16)
    rest = x - hi.astype(jnp.float32)
    mid = rest.astype(jnp.bfloat16)
    lo = (rest - mid.astype(jnp.float32)).astype(jnp.bfloat16)
    return hi, mid, lo


def east(x, w_ref, rim):
    rows = x.shape[0]
    parts = jnp.concatenate(split3(x), axis=0)
    p = jnp.dot(parts, w_ref[0], preferred_element_type=jnp.float32)
    q = jnp.dot(parts if rim else parts[:rows], w_ref[1], preferred_element_type=jnp.float32)
    out = q[:rows, :128] + p[2 * rows :, :128] + p[rows : 2 * rows, 128:]
    out = out + (p[rows : 2 * rows, :128] + p[:rows, 128:])
    out = out + p[:rows, :128]
    if not rim:
        return out, None
    return out, q[2 * rows :, 128:] + q[rows : 2 * rows, 128:] + q[:rows, 128:]


def side_rows(fields):
    return -(-len(fields) * LEV // 8) * 8


def places(fields):
    return [(lev * len(fields) + f,) * 2 for lev in range(LEV) for f in range(len(fields))]


def iota(shape, dim):
    return lax.broadcasted_iota(jnp.int32, shape, dim)


def north_parts(v, g):
    q5, q0 = g[5] * v[0], g[0] * v[5]
    a = q5 + g[10] * v[5] + g[9] * (v[4] + v[6]) + g[8] * (v[3] + v[7]) + g[7] * (v[2] + v[8]) + g[6] * (v[1] + v[9])
    b = q0 + g[1] * v[6] + g[2] * v[7] + g[3] * v[8] + g[4] * v[9]
    c = q5 + q0 + g[4] * v[1] + g[3] * v[2] + g[2] * v[3] + g[1] * v[4]
    return a, b, c


def north_chunk(fields, f_ref, kc, x_ref, g):
    row = iota((8, 128), 0)
    main, side = len(fields) * LEV * 8, side_rows(fields)
    used = sorted({a for pair in fields for a in pair if a is not None})

    def piece(lev, lt, lanes):
        x = {a: [f_ref[kc * (KC // 128) + lt, a, lev, pl.ds(o, 8, stride=RATIO), :] for o in range(RATIO)] for a in used}
        for f, (p, q) in enumerate(fields):
            v = x[p] if q is None else [x[p][o] * x[q][o] for o in range(RATIO)]
            a, b, c = north_parts(v, g)
            b = pltpu.roll(b, 1, 0)
            c = pltpu.roll(c, 7, 0)
            at = (lev * len(fields) + f) * 8
            x_ref[pl.ds(at, 8), lanes] = a + jnp.where(row == 0, 0.0, b) + jnp.where(row == 7, 0.0, c)
            up = main + lev * len(fields) + f
            x_ref[up : up + 1, lanes] = b[0:1]
            x_ref[up + side : up + side + 1, lanes] = c[7:8]

    for lev in range(LEV):
        for lt in range(KC // 128):
            piece(lev, lt, slice(lt * 128, lt * 128 + 128))


def selector(owner_ref):
    own = owner_ref[...].astype(jnp.float32)
    row = jnp.broadcast_to(jnp.concatenate([own, own], axis=1), (128, 128))
    col = row.T[:64]
    before = (col == row[:64]) & (iota((64, 128), 0) < (iota((64, 128), 1) & 63))
    rank = jnp.sum(before.astype(jnp.float32), axis=0, keepdims=True)
    slot = row[0:1] * 2.0 + rank
    where = iota((256, 128), 0).astype(jnp.float32)
    sel = (where == slot).astype(jnp.bfloat16)
    return jnp.concatenate([sel, sel[:, :64]], axis=1)


def pack_rim(fields, t_ref, edge, corner):
    lane = iota((8, 128), 1)
    row = iota((8, 128), 0)
    keep = (lane == 0) | (lane == LANE_LAST)
    packed = jnp.zeros((8, 128), jnp.float32)
    for at, sl in places(fields):
        v = jnp.where(keep, t_ref[at * 8 : at * 8 + 8, 128:256], 0.0)
        packed = packed + (pltpu.roll(v, sl, 1) if sl else v)
    edge[...] = packed
    rows = len(fields) * LEV * 8 + 2 * side_rows(fields)
    turned = t_ref[rows - 128 : rows, 128:256].T
    corner[...] = jnp.where(row == 0, turned[0:1], turned[LANE_LAST : LANE_LAST + 1])


def rim_copies(n_gx, n_gy, gx, gy, fields, t_ref, edge, corner, r_next, r_prev, r_side, r_corner, hsend, hrecv):
    east, west = lax.rem(gx + 1, n_gx), lax.rem(gx + n_gx - 1, n_gx)
    up, down = lax.rem(gy + 1, n_gy), lax.rem(gy + n_gy - 1, n_gy)
    main, n_side = len(fields) * LEV * 8, side_rows(fields)
    moves = (
        (t_ref.at[main : main + n_side, 0:128], r_next.at[:n_side], (gx, up)),
        (t_ref.at[main + n_side : main + 2 * n_side, 0:128], r_prev.at[:n_side], (gx, down)),
        (edge, r_side.at[0], (east, gy)),
        (edge, r_side.at[1], (west, gy)),
        (corner, r_corner.at[0], (east, up)),
        (corner, r_corner.at[1], (east, down)),
        (corner, r_corner.at[2], (west, up)),
        (corner, r_corner.at[3], (west, down)),
    )
    return [
        pltpu.make_async_remote_copy(s, d, hsend.at[i], hrecv.at[i], device_id=to, device_id_type=MESH)
        for i, (s, d, to) in enumerate(moves)
    ]


def rim_added(fields, t_ref, r_next, r_prev, r_side, r_corner):
    lane = iota((8, 128), 1)
    row = iota((8, 128), 0)
    keep = (lane == 0) | (lane == LANE_LAST)
    side = jnp.where(lane < LANE_LAST, r_side[0], r_side[1])
    n_side = side_rows(fields)
    first = lane < n_side
    secnd = (lane >= LANE_LAST) & (lane < LANE_LAST + n_side)
    corners = (
        (first, 0, 0, 2 * n_side % 128),
        (first, 7, 0, n_side),
        (secnd, 0, 1, (LANE_LAST + 2 * n_side) % 128),
        (secnd, 7, 1, (LANE_LAST + n_side) % 128),
    )
    for i, (lanes, at, got, turn) in enumerate(corners):
        v = jnp.broadcast_to(r_corner[i, got : got + 1], (8, 128))
        side = side + jnp.where(lanes & (row == at), pltpu.roll(v, turn, 1), 0.0)
    out = []
    for at, sl in places(fields):
        v = t_ref[at * 8 : at * 8 + 8, 0:128]
        v = v + jnp.where(row == 0, r_next[sl : sl + 1], 0.0) + jnp.where(row == 7, r_prev[sl : sl + 1], 0.0)
        out.append(v + jnp.where(keep, pltpu.roll(side, 128 - sl, 1) if sl else side, 0.0))
    return out


def slots(groups, sel, s_ref, m_ref):
    half = iota((32, 128), 1) < 64
    tiles = []
    for tt in range((groups + 1) // 2):
        st = s_ref[tt * 128 : tt * 128 + 128].T
        rt = pltpu.roll(st, 64, 1)
        left = [st[i * 32 : i * 32 + 32] for i in range(4)]
        right = [rt[i * 32 : i * 32 + 32] for i in range(4)]
        tiles.append((jnp.where(half, left[0], right[1]), jnp.where(half, left[2], right[3])))
        tiles.append((jnp.where(half, right[0], left[1]), jnp.where(half, right[2], left[3])))
    tiles = tiles[:groups]
    lhs = jnp.concatenate([jnp.concatenate([a, b], axis=1) for a, b in tiles], axis=0)
    lhs = jnp.concatenate(split3(lhs), axis=0)
    o = jnp.dot(lhs, m_ref[...], preferred_element_type=jnp.float32).astype(jnp.bfloat16)
    pay = []
    for part in range(3):
        for by in range(2):
            at = part * groups * 32
            pay.append(jnp.concatenate(
                [o[at + gg * 32 : at + gg * 32 + 32, by * 128 : by * 128 + 128] for gg in range(groups)], axis=1))
    return jnp.dot(sel, jnp.concatenate(pay, axis=0), preferred_element_type=jnp.float32)


def kernel(n_gx, n_gy, g, f_hbm, w_hbm, m_hbm, o_hbm, out_ref, f_ref, w_ref, m_ref, owner_ref, x_a, x_b, x_b1, t_a, t_b,
           mean_ref, s_a, s_b, src_a, src_b, dst_a, dst_b, edge, corner, r_next, r_prev, r_side, r_corner,
           fsem, wsem, msem, osem, ssem, rsem, hsend, hrecv, lsem):
    n = n_gx * n_gy
    gx, gy = lax.axis_index("gx"), lax.axis_index("gy")
    me = gx * n_gy + gy
    steps = w_ref.shape[0]
    per = KC // 128
    wide = FIRST * 64

    def f_copy(lt):
        return pltpu.make_async_copy(f_hbm.at[:, :, :, pl.ds(pl.multiple_of(lt * 128, 128), 128)], f_ref.at[lt], fsem.at[lt])

    def w_copy(kc):
        return pltpu.make_async_copy(w_hbm.at[kc], w_ref.at[kc], wsem.at[kc])

    def fetch(kc):
        for lt in range(per):
            f_copy(kc * per + lt).start()
        w_copy(kc).start()

    for kc in range(AHEAD):
        fetch(kc)
    m_copy = pltpu.make_async_copy(m_hbm, m_ref, msem)
    m_copy.start()
    o_copy = pltpu.make_async_copy(o_hbm, owner_ref, osem)
    o_copy.start()

    barrier = pltpu.get_barrier_semaphore()

    def greet(k, carry):
        d = lax.rem(me + k, n)
        pl.semaphore_signal(barrier, inc=1, device_id=d, device_id_type=LOGICAL)
        return carry

    lax.fori_loop(1, n, greet, 0, unroll=16)

    def local(fields, x_ref, t_ref, fresh, x_other=None):
        main = len(fields) * LEV * 8
        n_side = side_rows(fields)
        for ref in (x_ref, x_other):
            if ref is not None:
                ref[main : main + 2 * n_side] = jnp.zeros((2 * n_side, KC), jnp.float32)
        t_ref[...] = jnp.zeros_like(t_ref)

        def add(x, kc, rim):
            part, side = east(x[...], w_ref.at[kc], rim)
            t_ref[:, :128] += part
            if rim:
                t_ref[:, 128:] += side

        def chunk(kc, carry):
            for lt in range(per):
                f_copy(kc * per + lt).wait()
            pl.when(kc + AHEAD < steps)(lambda: fetch(kc + AHEAD))
            north_chunk(fields, f_ref, kc, x_ref, g)
            w_copy(kc).wait()
            rim = (kc == 0) | (kc == steps - 1)
            pl.when(rim)(lambda: add(x_ref, kc, True))
            pl.when(jnp.logical_not(rim))(lambda: add(x_ref, kc, False))
            return carry

        if fresh:
            lax.fori_loop(0, steps, chunk, 0)
        else:
            bufs = (x_ref, x_other)
            for kc in range(steps):
                north_chunk(fields, f_ref, kc, bufs[kc % 2], g)
                if kc:
                    add(bufs[(kc - 1) % 2], kc - 1, kc == 1)
            add(bufs[(steps - 1) % 2], steps - 1, True)
        side = t_ref[:, 128:]
        t_ref[:, 128:] = side + pltpu.roll(side, 127, 1) + pltpu.roll(side, 126, 1)

    def rims(i, fields, t_ref):
        bufs = (edge, corner, r_next, r_prev, r_side, r_corner, hsend, hrecv)
        return rim_copies(n_gx, n_gy, gx, gy, fields, t_ref, *(b.at[i] for b in bufs))

    def hand_over(i, src, dst):
        own = pltpu.make_async_copy(src.at[me], dst.at[me], lsem.at[i])
        own.start()

        def send(k, carry):
            d = lax.rem(me + lax.rem(k, 4) * (n // 4) + lax.rem(k // 4, 4) * (n // 16) + k // 16, n)
            pltpu.make_async_remote_copy(
                src.at[d], dst.at[me], ssem.at[i], rsem.at[i],
                device_id=d, device_id_type=LOGICAL,
            ).start()
            return carry

        lax.fori_loop(1, n, send, 0, unroll=8)
        return own

    local(ROUND_A, x_a, t_a, True)
    pack_rim(ROUND_A, t_a, edge.at[0], corner.at[0])
    pl.semaphore_wait(barrier, n - 1)
    copies_a = rims(0, ROUND_A, t_a)
    for copy in copies_a:
        copy.start()
    o_copy.wait()
    m_copy.wait()
    sel = selector(owner_ref)
    local(ROUND_B, x_b, t_b, False, x_b1)
    pack_rim(ROUND_B, t_b, edge.at[1], corner.at[1])
    copies_b = rims(1, ROUND_B, t_b)
    for copy in copies_b:
        copy.start()
    for copy in copies_a:
        copy.wait()
    got = rim_added(ROUND_A, t_a, r_next.at[0], r_prev.at[0], r_side.at[0], r_corner.at[0])
    for lev in range(LEV):
        for a in range(4):
            mean_ref[lev * 4 + a] = got[lev * len(ROUND_A) + a]
    for k in range(FIRST):
        for lev in range(LEV):
            p, q = PAIRS[k]
            s_a[(k * LEV + lev) * 8 : (k * LEV + lev) * 8 + 8] = (
                got[lev * len(ROUND_A) + 4 + k] - got[lev * len(ROUND_A) + p] * got[lev * len(ROUND_A) + q])
    src_a[...] = slots(FIRST // 2, sel, s_a, m_ref).reshape(n, 2, wide)
    own_a = hand_over(0, src_a, dst_a)

    for copy in copies_b:
        copy.wait()
    got = rim_added(ROUND_B, t_b, r_next.at[1], r_prev.at[1], r_side.at[1], r_corner.at[1])
    for k in range(len(ROUND_B)):
        for lev in range(LEV):
            p, q = ROUND_B[k]
            s_b[(k * LEV + lev) * 8 : (k * LEV + lev) * 8 + 8] = (
                got[lev * len(ROUND_B) + k] - mean_ref[lev * 4 + p] * mean_ref[lev * 4 + q])
    src_b[...] = slots(len(ROUND_B) // 2, sel, s_b, m_ref).reshape(n, 2, 640 - wide)
    own_b = hand_over(1, src_b, dst_b)

    rest = pl.ds(0, n - 1)
    own_a.wait()
    pltpu.make_async_copy(dst_a.at[rest], dst_a.at[rest], rsem.at[0]).wait()
    out_ref[:, :wide] = dst_a[...].reshape(2 * n, wide)
    own_b.wait()
    pltpu.make_async_copy(dst_b.at[rest], dst_b.at[rest], rsem.at[1]).wait()
    out_ref[:, wide:] = dst_b[...].reshape(2 * n, 640 - wide)
    pltpu.make_async_copy(src_a.at[rest], src_a.at[rest], ssem.at[0]).wait()
    pltpu.make_async_copy(src_b.at[rest], src_b.at[rest], ssem.at[1]).wait()


def per_device(fields, owner):
    n_gx, n_gy = lax.axis_size("gx"), lax.axis_size("gy")
    n = n_gx * n_gy
    taps = gauss_taps()
    g = [float(x) for x in taps]
    length = fields.shape[-1]
    weights = jnp.asarray(east_parts(east_matrix(length, taps)))
    blocks = jnp.asarray(block_matrix(), jnp.bfloat16)
    f32 = jnp.float32
    wide = FIRST * 64
    side = side_rows(ROUND_A)
    rows_a, rows_b = (len(r) * LEV * 8 + 2 * side_rows(r) for r in (ROUND_A, ROUND_B))
    return pl.pallas_call(
        functools.partial(kernel, n_gx, n_gy, g),
        out_shape=jax.ShapeDtypeStruct((2 * n, 640), f32),
        in_specs=[pl.BlockSpec(memory_space=pltpu.HBM)] * 4,
        out_specs=pl.BlockSpec(memory_space=pltpu.VMEM),
        scratch_shapes=[
            pltpu.VMEM((length // 128, 4, LEV, 80, 128), f32),
            pltpu.VMEM((length // KC, 2, KC, 256), jnp.bfloat16),
            pltpu.VMEM((256, 256), jnp.bfloat16),
            pltpu.VMEM((1, 64), jnp.int32),
            pltpu.VMEM((rows_a, KC), f32),
            pltpu.VMEM((rows_b, KC), f32),
            pltpu.VMEM((rows_b, KC), f32),
            pltpu.VMEM((rows_a, 256), f32),
            pltpu.VMEM((rows_b, 256), f32),
            pltpu.VMEM((4 * LEV, 8, 128), f32),
            pltpu.VMEM((-(-FIRST // 4) * 128, 128), f32),
            pltpu.VMEM((-(-len(ROUND_B) // 4) * 128, 128), f32),
            pltpu.VMEM((n, 2, wide), f32),
            pltpu.VMEM((n, 2, 640 - wide), f32),
            pltpu.VMEM((n, 2, wide), f32),
            pltpu.VMEM((n, 2, 640 - wide), f32),
            pltpu.VMEM((2, 8, 128), f32),
            pltpu.VMEM((2, 8, 128), f32),
            pltpu.VMEM((2, side, 128), f32),
            pltpu.VMEM((2, side, 128), f32),
            pltpu.VMEM((2, 2, 8, 128), f32),
            pltpu.VMEM((2, 4, 8, 128), f32),
            pltpu.SemaphoreType.DMA((length // 128,)),
            pltpu.SemaphoreType.DMA((length // KC,)),
            pltpu.SemaphoreType.DMA,
            pltpu.SemaphoreType.DMA,
            pltpu.SemaphoreType.DMA((2,)),
            pltpu.SemaphoreType.DMA((2,)),
            pltpu.SemaphoreType.DMA((2, 8)),
            pltpu.SemaphoreType.DMA((2, 8)),
            pltpu.SemaphoreType.DMA((2,)),
        ],
        compiler_params=pltpu.CompilerParams(
            collective_id=0, has_side_effects=True, vmem_limit_bytes=24 << 20
        ),
    )(*(pltpu.with_memory_space_constraint(x, pltpu.HBM) for x in (fields, weights, blocks, owner.reshape(1, 64))))


def solution(mesh):
    placed = (P(None, None, "gy", "gx"), P(("gx", "gy"), None))
    return jax.shard_map(
        per_device, mesh=mesh, in_specs=placed, out_specs=P(("gx", "gy"), None), check_vma=False
    )
```
